128 devices in a mesh: gx: 16 (over y, x), gy: 8 (over z, core).
Axes of the slice: x: 4, y: 4, z: 4, core: 2. Of those that a mesh axis runs over, the one named last changes fastest.
Arguments:
- state_now: float32 [128, 128, 4096], P(('gx', 'gy')), may hold values from -6 to 6
- state_prev: float32 [128, 128, 4096], P(('gx', 'gy')), may hold values from -6 to 6
- pml_flags: int32 [128], P(('gx', 'gy')), may hold values 0 or 1
- interfaces: int32 [256, 6], P(('gx', 'gy')), may hold values from -16 to 16, as said below
Outputs:
- new_state: float32 [128, 128, 4096], P(('gx', 'gy'))
- face_pressure: float32 [128, 6, 4096], P(('gx', 'gy'))
The draws below stay inside these ranges and needn't reach their ends.
Inputs may be any that keep to these rules, and one draw needn't show every extreme that they name: `interfaces`: column 0 and column 1 are always 0 (each device holds one box); column 1 names the box of the device one step further along gx and g = column 2 steps across gy; g is -1, 0 or 1 and that device exists whenever column 5 is 1. Columns 3 and 4 are offsets from -16 to 16. Column 5 is 0 exactly on the rows of the last index of gx, which join nothing, and 1 elsewhere.
All inputs are finite; a program needn't handle non-finite values. No bound on the sum of `pml_flags` on one device may be relied on, other than what follows from the above.
Results may differ from the reference program's by a relative error of at most 0.0003.
Values sent between devices are 32-bit elements; how exact they have to be, the bound alone decides.
A program may use at most 128 MiB of HBM per device.

```python
import math
import jax
import jax.numpy as jnp
from jax import lax

S0 = 128
S1 = 64
S2 = 64
BOX_DEV = 1
STEPS = 3
CROSS = 4096
OFF = 16
IF_DEV = 2
BOXES = 128
IFACES = 256
N_GX = 16
N_GY = 8


def draw_interfaces(key, part):
    row_count = IFACES
    subkeys = jax.random.split(jax.random.fold_in(key, 11), 5)
    row_ids = jnp.arange(row_count, dtype=jnp.int32)
    owners = row_ids // IF_DEV
    across_pos = owners % N_GY
    along_pos = owners // N_GY
    source_box = jax.random.randint(subkeys[0], (row_count,), 0, BOX_DEV).astype(jnp.int32)
    target_box = jax.random.randint(subkeys[1], (row_count,), 0, BOX_DEV).astype(jnp.int32)
    across_step = jax.random.randint(subkeys[2], (row_count,), -1, 2).astype(jnp.int32)
    across_step = jnp.clip(across_pos + across_step, 0, N_GY - 1) - across_pos
    first_displacement = jax.random.randint(subkeys[3], (row_count,), -OFF, OFF + 1).astype(jnp.int32)
    second_displacement = jax.random.randint(subkeys[4], (row_count,), -OFF, OFF + 1).astype(jnp.int32)
    first_displacement = first_displacement.at[0].set(-OFF)
    second_displacement = second_displacement.at[0].set(OFF)
    active = (along_pos < N_GX - 1).astype(jnp.int32)
    return jnp.stack([source_box, target_box, across_step, first_displacement, second_displacement, active], axis=1).astype(jnp.int32)


def place_ends(result, key, low, top_value):
    shape = result.shape
    index_at = [jax.random.randint(jax.random.fold_in(key, axis), (), 0, shape[axis]) for axis in range(len(shape))]
    result = result.at[tuple(index_at)].set(low)
    longest = shape.index(max(shape))
    index_at[longest] = (index_at[longest] + 1) % shape[longest]
    return result.at[tuple(index_at)].set(top_value)


def levels(stream_key, extent, cuts, smallest, largest):
    factor_of = 1.0
    for axis_at, blocks in cuts:
        steps = jax.random.uniform(jax.random.fold_in(jax.random.fold_in(stream_key, 6), axis_at), (blocks,), jnp.float32, smallest / len(cuts), largest / len(cuts))
        factor_of = factor_of * jnp.repeat(jnp.exp(steps), extent[axis_at] // blocks).reshape((-1,) + (1,) * (len(extent) - 1 - axis_at))
    return factor_of


def centred(stream_key, shape, spread, limit, shards=(), held_as=jnp.bfloat16):
    drawn = jax.random.normal(stream_key, shape, jnp.float32) * spread
    if len(shards) > 0:
        drawn = levels(stream_key, shape, shards, -0.22, 0.18) * drawn
    return jnp.clip(drawn, min=-limit, max=limit).astype(held_as)


def setup_inputs(seed: int = 0) -> dict:
    streams_of = jax.random.split(jax.random.key(seed), 5)
    return {
        "state_now": centred(streams_of[0], (BOXES, S0, CROSS), 1.0, 6.0, ((0, 128),), jnp.float32),
        "state_prev": centred(streams_of[1], (BOXES, S0, CROSS), 1.0, 6.0, ((0, 128),), jnp.float32),
        "pml_flags": place_ends((jax.random.randint(streams_of[2], (BOXES,), 0, 4) < 1).astype(jnp.int32), jax.random.fold_in(streams_of[2], 1), 0, 1),
        "interfaces": draw_interfaces(jax.random.fold_in(streams_of[4], 71), 0),
    }


COURANT = 0.4
DAMPING = 0.5
CENTER = -490.0 / 180.0
TOP_PRECISION = lax.Precision.HIGHEST

def cosine_basis(count):
    freqs = jnp.arange(count, dtype=jnp.float32)[:, None]
    cells = jnp.arange(count, dtype=jnp.float32)[None, :]
    weight = jnp.where(freqs == 0.0, jnp.sqrt(1.0 / count), jnp.sqrt(2.0 / count))
    return (weight * jnp.cos(math.pi * freqs * (cells + 0.5) / count)).astype(jnp.float32)

def face_rows():
    return jnp.array([0, 1, 2, S0 - 1, S0 - 2, S0 - 3], dtype=jnp.int32)

def coupling():
    return jnp.array([[1.5, -0.15, 1.0 / 90.0], [-0.15, 1.0 / 90.0, 0.0], [1.0 / 90.0, 0.0, 0.0]], dtype=jnp.float32)

def make_tables():
    basis_zero = cosine_basis(S0)
    basis_one = cosine_basis(S1)
    basis_two = cosine_basis(S2)
    face_basis = basis_zero[:, face_rows()]
    wave_zero = (math.pi * jnp.arange(S0, dtype=jnp.float32) / S0) ** 2
    wave_one = (math.pi * jnp.arange(S1, dtype=jnp.float32) / S1) ** 2
    wave_two = (math.pi * jnp.arange(S2, dtype=jnp.float32) / S2) ** 2
    wave = wave_zero[:, None, None] + wave_one[None, :, None] + wave_two[None, None, :]
    wave = wave.reshape(S0, S1 * S2)
    rooted = jnp.sqrt(wave)
    cosine = jnp.cos(COURANT * rooted)
    safe_wave = jnp.where(wave > 0.0, wave, 1.0)
    gain = jnp.where(wave > 0.0, 4.0 * jnp.sin(0.5 * COURANT * rooted) ** 2 / safe_wave, COURANT * COURANT)
    damping = DAMPING * ((jnp.arange(S0, dtype=jnp.float32) + 0.5) / S0) ** 2
    return (face_basis, basis_one, basis_two, cosine, gain, damping)

def cross_forward(slab, basis_one, basis_two):
    planes = slab.reshape(slab.shape[0], S1, S2)
    inner = jnp.einsum('rab,kb->rak', planes, basis_two, precision=TOP_PRECISION)
    outer = jnp.einsum('ja,rak->rjk', basis_one, inner, precision=TOP_PRECISION)
    return outer.reshape(slab.shape[0], S1 * S2)

def cross_inverse(slab, basis_one, basis_two):
    planes = slab.reshape(slab.shape[0], S1, S2)
    inner = jnp.einsum('rjk,kb->rjb', planes, basis_two, precision=TOP_PRECISION)
    outer = jnp.einsum('ja,rjb->rab', basis_one, inner, precision=TOP_PRECISION)
    return outer.reshape(slab.shape[0], S1 * S2)

def spectral_layers(values, tables):
    face_basis, basis_one, basis_two = (tables[0], tables[1], tables[2])
    coarse = jnp.einsum('kr,kc->rc', face_basis, values, precision=TOP_PRECISION)
    return cross_inverse(coarse, basis_one, basis_two)

def laplacian(values):
    volume = values.reshape(S0, S1, S2)
    padded = jnp.pad(volume, 3)
    summed = 3.0 * CENTER * volume
    for distance, factor in ((1, 1.5), (2, -0.15), (3, 1.0 / 90.0)):
        near = padded[3 + distance:3 + distance + S0, 3:3 + S1, 3:3 + S2] + padded[3 - distance:3 - distance + S0, 3:3 + S1, 3:3 + S2]
        near = near + padded[3:3 + S0, 3 + distance:3 + distance + S1, 3:3 + S2] + padded[3:3 + S0, 3 - distance:3 - distance + S1, 3:3 + S2]
        near = near + padded[3:3 + S0, 3:3 + S1, 3 + distance:3 + distance + S2] + padded[3:3 + S0, 3:3 + S1, 3 - distance:3 - distance + S2]
        summed = summed + factor * near
    return summed.reshape(S0, S1 * S2)

def modal_advance(current, previous, forcing, tables):
    face_basis, basis_one, basis_two, cosine, gain = (tables[0], tables[1], tables[2], tables[3], tables[4])
    slab_hat = cross_forward(forcing, basis_one, basis_two)
    forcing_hat = jnp.einsum('kr,rc->kc', face_basis, slab_hat, precision=TOP_PRECISION)
    return 2.0 * cosine * current - previous + gain * forcing_hat

def damped_advance(current, previous, forcing, tables):
    damping = tables[5]
    middle = jnp.zeros((S0 - 6, S1 * S2), jnp.float32)
    spread_force = jnp.concatenate([forcing[0:3], middle, forcing[3:6][::-1]], axis=0)
    rate = damping[:, None]
    return (2.0 * current - (1.0 - rate) * previous + COURANT * COURANT * (laplacian(current) + spread_force)) / (1.0 + rate)

def shift_face(layer, first_displacement, second_displacement):
    planes = layer.reshape(3, S1, S2)
    padded = jnp.pad(planes, ((0, 0), (OFF, OFF), (OFF, OFF)))
    start_one = (OFF - first_displacement).astype(jnp.int32)
    start_two = (OFF - second_displacement).astype(jnp.int32)
    moved = lax.dynamic_slice(padded, (jnp.zeros((), jnp.int32), start_one, start_two), (3, S1, S2))
    return moved.reshape(3, S1 * S2)

def reference(state_now, state_prev, pml_flags, interfaces):
    tables = make_tables()
    rows_face = face_rows()
    blend_weights = coupling()
    boxes_all = state_now.shape[0]

    def layers_one(packed):
        values, flag = packed
        return jnp.where(flag > 0, values[rows_face], spectral_layers(values, tables))

    def layers_all(current):
        return lax.map(layers_one, (current, pml_flags))

    def interface_forces(layers):

        def add_one(row_id, forces):
            row_id = jnp.asarray(row_id).astype(jnp.int32)
            entry = interfaces[row_id]
            owner = row_id // IF_DEV
            box_high = (owner * BOX_DEV + entry[0]).astype(jnp.int32)
            box_low = jnp.clip((owner + N_GY + entry[2]) * BOX_DEV + entry[1], 0, boxes_all - 1).astype(jnp.int32)
            active = entry[5].astype(jnp.float32)
            high_side = lax.dynamic_index_in_dim(layers, box_high, 0, keepdims=False)[3:6]
            lower_boundary_side = lax.dynamic_index_in_dim(layers, box_low, 0, keepdims=False)[0:3]
            toward_high = active * jnp.einsum('de,ec->dc', blend_weights, shift_face(lower_boundary_side, entry[3], entry[4]), precision=TOP_PRECISION)
            lowerward_direction = active * jnp.einsum('de,dc->ec', blend_weights, shift_face(high_side, -entry[3], -entry[4]), precision=TOP_PRECISION)
            forces = forces.at[box_high, 3:6].add(toward_high)
            forces = forces.at[box_low, 0:3].add(lowerward_direction)
            return forces
        return lax.fori_loop(0, IFACES, add_one, jnp.zeros_like(layers))

    def advance_one(packed):
        current, previous, forcing, flag = packed
        return jnp.where(flag > 0, damped_advance(current, previous, forcing, tables), modal_advance(current, previous, forcing, tables))
    current, previous = (state_now, state_prev)
    for repeat in range(STEPS):
        layers = layers_all(current)
        forces = interface_forces(layers)
        following = lax.map(advance_one, (current, previous, forces, pml_flags))
        previous, current = (current, following)
    return (current, layers_all(current))
```

```python
import math

import jax
import jax.numpy as jnp
import numpy as np
from jax import lax
from jax.experimental import pallas as pl
from jax.experimental.pallas import tpu as pltpu
from jax.sharding import PartitionSpec as P

S0 = 128
S1 = 64
S2 = 64
CROSS = S1 * S2
STEPS = 3
TILES = CROSS // 128
PLANE = 32
MESH = pl.DeviceIdType.MESH
F32 = jnp.float32
BF16 = jnp.bfloat16
HIGHEST = lax.Precision.HIGHEST

COURANT2 = 0.16
CENTER3 = 3.0 * (-490.0 / 180.0)
TAPS = (1.5, -0.15, 1.0 / 90.0)
PAIRS = {(0, 0): 0, (0, 1): 1, (0, 2): 2, (1, 1): 3, (1, 2): 4, (2, 2): 5}


def basis(n):
    k = np.arange(n)[:, None]
    i = np.arange(n)[None, :]
    weight = np.where(k == 0, math.sqrt(1.0 / n), math.sqrt(2.0 / n))
    return weight * np.cos(math.pi * k * (i + 0.5) / n)


def twice(a):
    n = a.shape[0]
    out = np.zeros((2 * n, 2 * n))
    out[:n, :n] = a
    out[n:, n:] = a
    return out


def halves(a):
    high = a.astype(np.float32).astype(BF16)
    low = (a - high.astype(np.float64)).astype(np.float32).astype(BF16)
    return high, low


def constants():
    c0, c1 = basis(S0), basis(S1)
    k = (math.pi * np.arange(S0) / S0) ** 2
    a = (math.pi * np.arange(S1) / S1) ** 2
    wave = (k[:, None, None] + a[None, :, None] + a[None, None, :]).reshape(S0, CROSS)
    safe = np.where(wave > 0, wave, 1.0)
    gain = np.where(wave > 0, 4.0 * np.sin(0.2 * np.sqrt(wave)) ** 2 / safe, COURANT2)
    face = c0[:, :3]
    sign = (-1.0) ** np.arange(S0)
    planes = []
    for s in (np.ones(S0), sign):
        for d, e in PAIRS:
            planes.append(((face[:, d] * face[:, e] * s) @ gain).reshape(PLANE, 128))
    order = np.concatenate([np.arange(0, S1, 2), np.arange(1, S1, 2)])
    c1p = c1[order][:, order]
    misc = np.concatenate(
        [np.repeat(face[:, d : d + 1], 128, axis=1) for d in range(3)]
        + planes
        + [twice(c1), twice(c1.T), twice(c1p), twice(c1p.T)],
        axis=0,
    )

    def band(n):
        out = np.zeros((n, n))
        for distance, tap in enumerate(TAPS, 1):
            out += tap * (np.eye(n, k=distance) + np.eye(n, k=-distance))
        return out

    along_hi, along_lo = halves(band(S0))
    inner_hi, inner_lo = halves(twice(twice(band(S2))))
    stencil = np.concatenate(
        [np.concatenate([along_hi, along_lo], axis=1), inner_hi, inner_lo], axis=0
    )
    return gain.astype(np.float32), misc.astype(np.float32), stencil


ROW_FACE, ROW_P, ROW_C = 0, 384, 768


def rate_of(row):
    return 0.5 * ((row + 0.5) / S0) ** 2


FACE_COEF = [COURANT2 / (1.0 + rate_of(i)) for i in (0, 1, 2, 127, 126, 125)]


def split(x):
    high = x.astype(BF16)
    return high, (x - high.astype(F32)).astype(BF16)


def dot(a, b):
    return jnp.dot(a, b, preferred_element_type=F32)


def top_dot(a, b):
    return jnp.dot(a, b, preferred_element_type=F32, precision=HIGHEST)


def couple(p):
    w1, w2, w3 = TAPS
    return [w1 * p[0] + w2 * p[1] + w3 * p[2], w2 * p[0] + w3 * p[1], w3 * p[0]]


def kernel(
    flags, faces, now_hbm, prev_hbm, gain_hbm, misc_hbm, stencil_hbm,
    out, layers_out,
    state, gain, slow, misc, stencil, halved, rolled, rows,
    acc, picked, spread, free, left, right, flag_out, flag_in, layers, sums, low_in, force_in, outp,
    load_sem, send_sem, recv_sem,
):
    gx, gy = lax.axis_index("gx"), lax.axis_index("gy")
    nx, ny = lax.axis_size("gx"), lax.axis_size("gy")
    inner = pl.ds(128, CROSS)

    loads = [
        pltpu.make_async_copy(misc_hbm, misc, load_sem.at[0]),
        pltpu.make_async_copy(now_hbm.at[0], state.at[0, :, inner], load_sem.at[1]),
        pltpu.make_async_copy(stencil_hbm, stencil, load_sem.at[2]),
        pltpu.make_async_copy(prev_hbm.at[0], state.at[1, :, inner], load_sem.at[3]),
        pltpu.make_async_copy(gain_hbm, gain, load_sem.at[4]),
    ]
    for load in loads:
        load.start()

    low_in[...] = jnp.zeros_like(low_in)
    force_in[...] = jnp.zeros_like(force_in)
    flag_in[...] = jnp.zeros_like(flag_in)
    flag_out[...] = jnp.full(flag_out.shape, flags[0], jnp.int32).astype(F32)

    back_ok, ahead_ok = gx > 0, gx < nx - 1
    side_ok = {-1: gy > 0, 0: gy >= 0, 1: gy < ny - 1}
    barrier = pltpu.get_barrier_semaphore()
    for ok, to_x in ((back_ok, gx - 1), (ahead_ok, gx + 1)):
        for side in (-1, 0, 1):

            @pl.when(jnp.logical_and(ok, side_ok[side]))
            def _():
                pl.semaphore_signal(barrier, inc=1, device_id=(to_x, gy + side), device_id_type=MESH)

    sides = 1 + (gy > 0).astype(jnp.int32) + (gy < ny - 1).astype(jnp.int32)
    ends = (gx > 0).astype(jnp.int32) + (gx < nx - 1).astype(jnp.int32)
    pl.semaphore_wait(barrier, sides * ends)

    def back(source, target, sem, g):
        return pltpu.make_async_remote_copy(
            src_ref=source, dst_ref=target, send_sem=send_sem.at[sem], recv_sem=recv_sem.at[sem],
            device_id=(gx - 1, gy - g), device_id_type=MESH,
        )

    def ahead(source, target, sem, g):
        return pltpu.make_async_remote_copy(
            src_ref=source, dst_ref=target, send_sem=send_sem.at[sem], recv_sem=recv_sem.at[sem],
            device_id=(gx + 1, gy + g), device_id_type=MESH,
        )

    def flag_copy(g):
        return back(flag_out, flag_in.at[g + 1], g + 1, g)

    def low_copy(n, g):
        return back(layers.at[n, pl.ds(0, 96)], low_in.at[n, g + 1], 3 + 3 * n + g + 1, g)

    def force_copy(n, g):
        return ahead(sums.at[n, g + 1], force_in.at[n, g + 1], 12 + 3 * n + g + 1, g)

    def send_back(copy):
        for g in (-1, 0, 1):

            @pl.when(jnp.logical_and(back_ok, side_ok[-g]))
            def _():
                copy(g).start()

    def got_back(copy):
        for g in (-1, 0, 1):

            @pl.when(jnp.logical_and(ahead_ok, side_ok[g]))
            def _():
                copy(g).wait_recv()

    def send_ahead(copy):
        for g in (-1, 0, 1):

            @pl.when(jnp.logical_and(ahead_ok, side_ok[g]))
            def _():
                copy(g).start()

    def got_ahead(copy):
        for g in (-1, 0, 1):

            @pl.when(jnp.logical_and(back_ok, side_ok[-g]))
            def _():
                copy(g).wait_recv()

    send_back(flag_copy)

    def is_pml(shape):
        return jnp.full(shape, flags[0], jnp.int32) > 0

    lanes = lax.broadcasted_iota(jnp.int32, (PLANE, 128), 1)
    first = lanes < 64

    def fb(d):
        return misc[ROW_FACE + d * 128 : ROW_FACE + (d + 1) * 128, :].reshape(16, 8, 128)

    def note_faces(block, c):
        tiles = block.reshape(16, 8, 128)
        for d in range(3):
            acc[pl.ds(d * 256 + c, 8, stride=PLANE), :] = jnp.sum(fb(d) * tiles, axis=0)
        picked[pl.ds(c, 8, stride=PLANE), :] = block[0:8, :]
        picked[pl.ds(256 + c, 8, stride=PLANE), :] = block[120:128, :]

    def gathered_faces():
        low, high = [], []
        pml = is_pml((PLANE, 128))
        for d in range(3):
            part = [acc[d * 256 + s * 32 : d * 256 + (s + 1) * 32, :] for s in range(8)]
            even = (part[0] + part[2]) + (part[4] + part[6])
            odd = (part[1] + part[3]) + (part[5] + part[7])
            row_low = picked[d * 32 : (d + 1) * 32, :]
            row_high = picked[256 + (7 - d) * 32 : 256 + (8 - d) * 32, :]
            low.append(jnp.where(pml, row_low, even + odd))
            high.append(jnp.where(pml, row_high, even - odd))
        return low + high

    loads[0].wait()
    loads[1].wait()

    def tile(c):
        return pl.ds(pl.multiple_of(c * 128, 128), 128)

    @pl.loop(0, TILES // 2)
    def _(t):
        for h in range(2):
            c = 2 * t + h
            note_faces(state[0, :, tile(c + 1)], c)

    for e, plane in enumerate(gathered_faces()):
        layers[0, e * 32 : (e + 1) * 32, :] = plane
    send_back(lambda g: low_copy(0, g))

    got_back(flag_copy)
    big_row = lax.broadcasted_iota(jnp.int32, (128, 128), 0)
    big_col = lax.broadcasted_iota(jnp.int32, (128, 128), 1)
    same = (big_row >> 6) == (big_col >> 6)
    eye = jnp.where(big_row == big_col, 1.0, 0.0).astype(F32)
    own = is_pml((128, 128))
    ours, ours_t, ours_p, ours_pt = (
        jnp.where(own, eye, misc[ROW_C + i * 128 : ROW_C + (i + 1) * 128, :]) for i in range(4)
    )

    def theirs(r):
        g = jnp.full((8, 128), faces[r, 2], jnp.int32)
        value = jnp.where(g == -1, flag_in[0], jnp.where(g == 0, flag_in[1], flag_in[2]))
        return jnp.broadcast_to(value[0:1, :], (128, 128)) > 0.5

    their = [theirs(r) for r in range(2)]
    q_row, q_col = big_row & 63, big_col & 63
    j_row = 2 * (q_row & 31) + (q_row >> 5)
    j_col = 2 * (q_col & 31) + (q_col >> 5)
    upper = big_row < 64
    step_one = jnp.where(
        upper,
        jnp.full((128, 128), faces[0, 3], jnp.int32),
        jnp.full((128, 128), faces[1, 3], jnp.int32),
    )
    shift_one = jnp.where(jnp.logical_and(same, j_col == j_row - step_one), 1.0, 0.0).astype(F32)
    their_pt = jnp.where(
        jnp.where(upper, their[0].astype(F32), their[1].astype(F32)) > 0.5,
        eye,
        misc[ROW_C + 3 * 128 : ROW_C + 4 * 128, :],
    )
    cross_one = top_dot(ours_p, top_dot(shift_one, their_pt))

    def keep_left(i, matrix):
        hi, lo = split(matrix)
        left[i, :, 0:128] = hi
        left[i, :, 128:256] = hi
        left[i, :, 256:384] = lo

    def keep_right(i, matrix):
        hi, lo = split(matrix)
        right[i, 0:128, :] = hi
        right[i, 128:256, :] = hi
        right[i, 256:384, :] = lo

    keep_left(0, cross_one)
    keep_left(1, cross_one.T)
    for r in range(2):
        step_two = jnp.full((128, 128), faces[r, 4], jnp.int32)
        shift_two = jnp.where(jnp.logical_and(same, q_row == q_col - step_two), 1.0, 0.0).astype(F32)
        their_c = jnp.where(their[r], eye, misc[ROW_C : ROW_C + 128, :])
        cross_two = top_dot(their_c, top_dot(shift_two, ours_t))
        keep_right(r, cross_two)
        keep_right(2 + r, cross_two.T)
    keep_left(2, ours_pt)
    keep_right(4, ours)

    def chosen(r, g):
        hit = jnp.logical_and(
            jnp.full((96, 128), faces[r, 2], jnp.int32) == g,
            jnp.full((96, 128), faces[r, 5], jnp.int32) > 0,
        )
        return hit

    def stacked(x):
        hi, lo = split(x)
        return jnp.concatenate([hi, lo, hi], axis=1)

    def columns(first_rows, second_rows):
        outer = []
        for w in (first_rows, second_rows):
            even, odd = [], []
            for e in range(3):
                p = w[e * 32 : (e + 1) * 32, :]
                swapped = pltpu.roll(p, 64, 1)
                even.append(jnp.where(first, p, swapped))
                odd.append(jnp.where(first, swapped, p))
            outer.append(jnp.concatenate(even, axis=1))
            outer.append(jnp.concatenate(odd, axis=1))
        hi, lo = split(jnp.concatenate(outer, axis=0))
        return jnp.concatenate([hi, lo, hi], axis=0)

    def planes_of(product, s):
        top = product[64 * s : 64 * s + 32, :]
        bottom = product[64 * s + 32 : 64 * s + 64, :]
        return [
            jnp.where(first, top[:, e * 128 : (e + 1) * 128], bottom[:, e * 128 : (e + 1) * 128])
            for e in range(3)
        ]

    def make_sums(n):
        z = couple([layers[n, (3 + d) * 32 : (4 + d) * 32, :] for d in range(3)])
        z3 = stacked(jnp.concatenate(z, axis=0))
        product = dot(left[1], columns(dot(z3, right[2]), dot(z3, right[3])))
        moved = [jnp.concatenate(planes_of(product, r), axis=0) for r in range(2)]
        for g in (-1, 0, 1):
            total = jnp.where(chosen(0, g), moved[0], 0.0) + jnp.where(chosen(1, g), moved[1], 0.0)
            sums[n, g + 1] = total

    def high_force(n):
        parts = []
        for r in range(2):
            pick = jnp.zeros((96, 128), F32)
            for g in (-1, 0, 1):
                pick = jnp.where(chosen(r, g), low_in[n, g + 1], pick)
            parts.append(dot(stacked(pick), right[r]))
        product = dot(left[0], columns(parts[0], parts[1]))
        a, b = planes_of(product, 0), planes_of(product, 1)
        return couple([x + y for x, y in zip(a, b)])

    def response(force):
        pml = is_pml((PLANE, 128))
        low, high = [], []
        for d in range(3):
            near, far = 0.0, 0.0
            for e in range(3):
                i = PAIRS[(min(d, e), max(d, e))]
                p = misc[ROW_P + i * 32 : ROW_P + (i + 1) * 32, :]
                q = misc[ROW_P + 192 + i * 32 : ROW_P + 192 + (i + 1) * 32, :]
                near = near + (p * force[e] + q * force[3 + e])
                far = far + (q * force[e] + p * force[3 + e])
            low.append(jnp.where(pml, FACE_COEF[d] * force[d], near))
            high.append(jnp.where(pml, FACE_COEF[3 + d] * force[3 + d], far))
        return low + high

    make_sums(0)
    send_ahead(lambda g: force_copy(0, g))

    k = big_row.astype(F32)
    rate = 0.5 * ((k + 0.5) * (1.0 / S0)) ** 2
    inverse = 1.0 / (1.0 + rate)
    rows[0] = jnp.where(own, (2.0 + COURANT2 * CENTER3) * inverse, 2.0)
    rows[1] = jnp.where(own, (1.0 - rate) * inverse, 1.0)
    rows[2] = jnp.where(own, COURANT2 * inverse, 0.0)
    edge = jnp.zeros((S0, 128), F32)
    for b in range(2):
        state[b, :, 0:128] = edge
        state[b, :, 128 + CROSS : 256 + CROSS] = edge
    for c in (0, 1, TILES + 2, TILES + 3):
        rolled[:, c * 128 : (c + 1) * 128] = edge
    spread[...] = jnp.zeros_like(spread)
    loads[4].wait()

    @pl.loop(0, TILES)
    def _(c):
        col = c * 128 + big_col
        mode_a = (col >> 6).astype(F32) * (math.pi / S1)
        mode_b = (col & 63).astype(F32) * (math.pi / S2)
        mode_k = k * (math.pi / S0)
        masked = jnp.where(own, 0.0, gain[:, tile(c)])
        gain[:, tile(c)] = masked
        slow[:, tile(c)] = masked * (mode_k * mode_k + mode_a * mode_a + mode_b * mode_b)

    loads[2].wait()
    loads[3].wait()

    alternate = (lax.broadcasted_iota(jnp.int32, (8, 128), 0) & 1) == 0

    def forced(block, c):
        total = None
        for d in range(3):
            plus = jnp.broadcast_to(outp[pl.ds(d * 32 + c, 1), :], (8, 128))
            minus = jnp.broadcast_to(outp[pl.ds(96 + d * 32 + c, 1), :], (8, 128))
            term = fb(d) * jnp.where(alternate, plus, minus)[None]
            total = term if total is None else total + term
        block = block + gain[:, tile(c)] * total.reshape(128, 128)
        top = block[0:8, :] + spread[pl.ds(c, 8, stride=PLANE), :]
        bottom = block[120:128, :] + spread[pl.ds(256 + c, 8, stride=PLANE), :]
        return jnp.concatenate([top, block[8:120, :], bottom], axis=0)

    def keep_force(force):
        pml = is_pml((PLANE, 128))
        for d in range(3):
            outp[d * 32 : (d + 1) * 32, :] = force[d] + force[3 + d]
            outp[96 + d * 32 : 96 + (d + 1) * 32, :] = force[d] - force[3 + d]
            spread[d * 32 : (d + 1) * 32, :] = jnp.where(pml, FACE_COEF[d] * force[d], 0.0)
            at = 256 + (7 - d) * 32
            spread[at : at + 32, :] = jnp.where(pml, FACE_COEF[3 + d] * force[3 + d], 0.0)

    def finish_state(b, n):
        @pl.loop(0, TILES // 2)
        def _(t):
            for h in range(2):
                c = 2 * t + h
                block = state[b, :, tile(c + 1)]
                if n > 0:
                    block = forced(block, c)
                    state[b, :, tile(c + 1)] = block
                hi, lo = split(block)
                halved[0:128, tile(c)] = hi
                halved[128:256, tile(c)] = lo
                rolled[:, tile(c + 2)] = pltpu.roll(block, 64, 1)

    w1, w2, w3 = TAPS
    big_first = big_col < 64

    def advance(b, p):
        @pl.loop(0, TILES // 2)
        def _(t):
            wide = pl.ds(pl.multiple_of(t * 256, 256), 256)
            pair = halved[:, wide]
            hi, lo = pair[0:128, :], pair[128:256, :]
            along = stencil[0:128, :]
            twice_hi = jnp.concatenate([along[:, 0:128], along[:, 0:128]], axis=1)
            taps = dot(twice_hi, pair) + dot(along[:, 128:256], hi)
            taps += dot(hi, stencil[128:384, :]) + dot(lo, stencil[128:384, :])
            taps += dot(hi, stencil[384:640, :])
            ring = [rolled[:, tile(2 * t + i)] for i in range(6)]
            quads = [w1 * (ring[i + 2] + ring[i + 1]) + w3 * (ring[i + 3] + ring[i]) for i in range(3)]
            for h in range(2):
                c = 2 * t + h
                block = state[b, :, tile(c + 1)]
                sides_ = state[b, :, tile(c)] + state[b, :, tile(c + 2)]
                stencil_sum = taps[:, h * 128 : (h + 1) * 128] + w2 * sides_
                stencil_sum += jnp.where(big_first, quads[h], quads[h + 1])
                following = (rows[0] - slow[:, tile(c)]) * block - rows[1] * state[p, :, tile(c + 1)]
                following += rows[2] * stencil_sum
                state[p, :, tile(c + 1)] = following
                note_faces(following, c)

        for e, plane in enumerate(gathered_faces()):
            free[e * 32 : (e + 1) * 32, :] = plane

    for n in range(STEPS):
        b, p = n % 2, 1 - n % 2
        if n > 0:
            send_back(lambda g: low_copy(n, g))
            make_sums(n)
            send_ahead(lambda g: force_copy(n, g))
        finish_state(b, n)
        advance(b, p)
        got_back(lambda g: low_copy(n, g))
        high = high_force(n)
        got_ahead(lambda g: force_copy(n, g))
        low = [
            force_in[n, 0, e * 32 : (e + 1) * 32, :]
            + force_in[n, 1, e * 32 : (e + 1) * 32, :]
            + force_in[n, 2, e * 32 : (e + 1) * 32, :]
            for e in range(3)
        ]
        force = low + high
        for e, plane in enumerate(response(force)):
            at = slice(e * 32, (e + 1) * 32)
            layers[n + 1, at, :] = free[at, :] + plane
        keep_force(force)

    last = STEPS % 2

    @pl.loop(0, TILES // 2)
    def _(t):
        for h in range(2):
            c = 2 * t + h
            out[0, :, tile(c)] = forced(state[last, :, tile(c + 1)], c)

    final = layers[STEPS]
    turned = dot(stacked(final), right[4])
    product = dot(left[2], columns(turned[0:96, :], turned[96:192, :]))
    for s in range(2):
        for e, plane in enumerate(planes_of(product, s)):
            at = (3 * s + e) * 32
            outp[at : at + 32, :] = plane

    @pl.loop(0, TILES)
    def _(c):
        layers_out[0, :, tile(c)] = outp[pl.ds(c, 8, stride=PLANE), :][0:6, :]

    for g in (-1, 0, 1):

        @pl.when(jnp.logical_and(back_ok, side_ok[-g]))
        def _():
            flag_copy(g).wait_send()
            for n in range(STEPS):
                low_copy(n, g).wait_send()

        @pl.when(jnp.logical_and(ahead_ok, side_ok[g]))
        def _():
            for n in range(STEPS):
                force_copy(n, g).wait_send()


def local(state_now, state_prev, pml_flags, interfaces):
    gain, misc, stencil = constants()
    smem = pl.BlockSpec(memory_space=pltpu.SMEM)
    hbm = pl.BlockSpec(memory_space=pl.ANY)
    vmem = pl.BlockSpec(memory_space=pltpu.VMEM)
    return pl.pallas_call(
        kernel,
        out_shape=(
            jax.ShapeDtypeStruct((1, S0, CROSS), F32),
            jax.ShapeDtypeStruct((1, 6, CROSS), F32),
        ),
        in_specs=[smem, smem, hbm, hbm, hbm, hbm, hbm],
        out_specs=(vmem, vmem),
        scratch_shapes=[
            pltpu.VMEM((2, S0, CROSS + 256), F32),
            pltpu.VMEM((S0, CROSS), F32),
            pltpu.VMEM((S0, CROSS), F32),
            pltpu.VMEM(misc.shape, F32),
            pltpu.VMEM(stencil.shape, BF16),
            pltpu.VMEM((256, CROSS), BF16),
            pltpu.VMEM((S0, CROSS + 512), F32),
            pltpu.VMEM((3, 128, 128), F32),
            pltpu.VMEM((768, 128), F32),
            pltpu.VMEM((512, 128), F32),
            pltpu.VMEM((512, 128), F32),
            pltpu.VMEM((192, 128), F32),
            pltpu.VMEM((3, 128, 384), BF16),
            pltpu.VMEM((5, 384, 128), BF16),
            pltpu.VMEM((8, 128), F32),
            pltpu.VMEM((3, 8, 128), F32),
            pltpu.VMEM((STEPS + 1, 192, 128), F32),
            pltpu.VMEM((STEPS, 3, 96, 128), F32),
            pltpu.VMEM((STEPS, 3, 96, 128), F32),
            pltpu.VMEM((STEPS, 3, 96, 128), F32),
            pltpu.VMEM((256, 128), F32),
            pltpu.SemaphoreType.DMA((5,)),
            pltpu.SemaphoreType.DMA((21,)),
            pltpu.SemaphoreType.DMA((21,)),
        ],
        compiler_params=pltpu.CompilerParams(
            collective_id=0, has_side_effects=True, vmem_limit_bytes=56 * 1024 * 1024
        ),
    )(pml_flags, interfaces, state_now, state_prev, jnp.asarray(gain), jnp.asarray(misc), jnp.asarray(stencil))


def solution(mesh):
    one, two, three = P(("gx", "gy")), P(("gx", "gy"), None), P(("gx", "gy"), None, None)
    return jax.shard_map(
        local,
        mesh=mesh,
        in_specs=(three, three, one, two),
        out_specs=(three, three),
        check_vma=False,
    )
```

```python
import math

import jax
import jax.numpy as jnp
import numpy as np
from jax import lax
from jax.experimental import pallas as pl
from jax.experimental.pallas import tpu as pltpu
from jax.sharding import PartitionSpec as P

S0 = 128
S1 = 64
S2 = 64
CROSS = S1 * S2
STEPS = 3
TILES = CROSS // 128
PLANE = 32
MESH = pl.DeviceIdType.MESH
F32 = jnp.float32
BF16 = jnp.bfloat16

COURANT2 = 0.16
CENTER3 = 3.0 * (-490.0 / 180.0)
TAPS = (1.5, -0.15, 1.0 / 90.0)
TAPS_90 = (135.0, -13.5, 1.0)
PAIRS = {(0, 0): 0, (0, 1): 1, (0, 2): 2, (1, 1): 3, (1, 2): 4, (2, 2): 5}


def basis(n):
    k = np.arange(n)[:, None]
    i = np.arange(n)[None, :]
    weight = np.where(k == 0, math.sqrt(1.0 / n), math.sqrt(2.0 / n))
    return weight * np.cos(math.pi * k * (i + 0.5) / n)


def twice(a):
    n = a.shape[0]
    out = np.zeros((2 * n, 2 * n))
    out[:n, :n] = a
    out[n:, n:] = a
    return out


def constants():
    c0, c1 = basis(S0), basis(S1)
    k = (math.pi * np.arange(S0) / S0) ** 2
    a = (math.pi * np.arange(S1) / S1) ** 2
    wave = (k[:, None, None] + a[None, :, None] + a[None, None, :]).reshape(S0, CROSS)
    safe = np.where(wave > 0, wave, 1.0)
    gain = np.where(wave > 0, 4.0 * np.sin(0.2 * np.sqrt(wave)) ** 2 / safe, COURANT2)
    face = c0[:, :3]
    sign = (-1.0) ** np.arange(S0)
    planes = []
    for s in (np.ones(S0), sign):
        for d, e in PAIRS:
            planes.append(((face[:, d] * face[:, e] * s) @ gain).reshape(PLANE, 128))
    order = np.concatenate([np.arange(0, S1, 2), np.arange(1, S1, 2)])
    c1p = c1[order][:, order]
    misc = np.concatenate(
        [np.repeat(face[:, d : d + 1], 128, axis=1) for d in range(3)]
        + planes
        + [twice(c1), twice(c1.T), twice(c1p), twice(c1p.T)],
        axis=0,
    )

    def band(n):
        out = np.zeros((n, n))
        for distance, tap in enumerate(TAPS_90, 1):
            out += tap * (np.eye(n, k=distance) + np.eye(n, k=-distance))
        return out

    along = band(S0)
    stencil = np.concatenate([np.concatenate([along, along], axis=1), twice(twice(band(S2)))], axis=0)
    return gain.astype(np.float32), misc.astype(np.float32), stencil.astype(BF16)


ROW_FACE, ROW_P, ROW_C = 0, 384, 768


def rate_of(row):
    return 0.5 * ((row + 0.5) / S0) ** 2


FACE_COEF = [COURANT2 / (1.0 + rate_of(i)) for i in (0, 1, 2, 127, 126, 125)]


def split(x):
    high = x.astype(BF16)
    return high, (x - high.astype(F32)).astype(BF16)


def dot(a, b):
    return jnp.dot(a, b, preferred_element_type=F32)


def couple(p):
    w1, w2, w3 = TAPS
    return [w1 * p[0] + w2 * p[1] + w3 * p[2], w2 * p[0] + w3 * p[1], w3 * p[0]]


def stacked(x):
    hi, lo = split(x)
    return jnp.concatenate([hi, lo, hi], axis=1)


def first_half():
    return lax.broadcasted_iota(jnp.int32, (PLANE, 128), 1) < 64


def columns(*sets):
    first = first_half()
    outer = []
    for w in sets:
        even, odd = [], []
        for e in range(3):
            p = w[e * 32 : (e + 1) * 32, :]
            swapped = pltpu.roll(p, 64, 1)
            even.append(jnp.where(first, p, swapped))
            odd.append(jnp.where(first, swapped, p))
        outer.append(jnp.concatenate(even, axis=1))
        outer.append(jnp.concatenate(odd, axis=1))
    hi, lo = split(jnp.concatenate(outer, axis=0))
    return jnp.concatenate([hi, lo, hi], axis=0)


def planes_of(product, s):
    first = first_half()
    top = product[64 * s : 64 * s + 32, :]
    bottom = product[64 * s + 32 : 64 * s + 64, :]
    return [
        jnp.where(first, top[:, e * 128 : (e + 1) * 128], bottom[:, e * 128 : (e + 1) * 128])
        for e in range(3)
    ]


def left_form(matrix):
    hi, lo = split(matrix)
    return jnp.concatenate([hi, hi, lo], axis=1)


def right_form(matrix):
    hi, lo = split(matrix)
    return jnp.concatenate([hi, hi, lo], axis=0)


def exchange(
    flags, faces_hbm, now_hbm, prev_hbm, gain_hbm, misc_hbm, stencil_hbm,
    free_out, pack_out,
    state, gain, slow, misc, stencil, halved, rolled, rows,
    acc, picked, free, left, right, flag_out, flag_in, layers, sums, low_in, force_in, pack,
    faces, load_sem, send_sem, recv_sem, out_sem,
):
    gx, gy = lax.axis_index("gx"), lax.axis_index("gy")
    nx, ny = lax.axis_size("gx"), lax.axis_size("gy")

    back_ok, ahead_ok = gx > 0, gx < nx - 1
    side_ok = {-1: gy > 0, 0: gy >= 0, 1: gy < ny - 1}
    barrier = pltpu.get_barrier_semaphore()
    for ok, to_x in ((back_ok, gx - 1), (ahead_ok, gx + 1)):
        for side in (-1, 0, 1):

            @pl.when(jnp.logical_and(ok, side_ok[side]))
            def _():
                pl.semaphore_signal(barrier, inc=1, device_id=(to_x, gy + side), device_id_type=MESH)

    head = pltpu.make_async_copy(misc_hbm, misc, load_sem.at[0])
    head.start()
    listed = pltpu.make_async_copy(faces_hbm, faces, load_sem.at[8])
    listed.start()
    chunk = CROSS // 4
    nows = [
        pltpu.make_async_copy(
            now_hbm.at[0, :, pl.ds(i * chunk, chunk)],
            state.at[0, :, pl.ds(128 + i * chunk, chunk)],
            load_sem.at[4 + i],
        )
        for i in range(4)
    ]
    for load in nows:
        load.start()
    rest = [
        pltpu.make_async_copy(gain_hbm, gain, load_sem.at[1]),
        pltpu.make_async_copy(prev_hbm.at[0], state.at[1, :, pl.ds(128, CROSS)], load_sem.at[2]),
        pltpu.make_async_copy(stencil_hbm, stencil, load_sem.at[3]),
    ]
    for load in rest:
        load.start()
    flag_out[...] = jnp.full(flag_out.shape, flags[0], jnp.int32).astype(F32)

    core = lax.rem(gy, 2)
    away = 2 * core - 1
    away_ok = jnp.where(core == 0, gy > 0, gy < ny - 1)
    order = ((away, away_ok), (-away, gy >= 0), (0, gy >= 0))

    def back(source, target, sem, g):
        return pltpu.make_async_remote_copy(
            src_ref=source, dst_ref=target, send_sem=send_sem.at[sem], recv_sem=recv_sem.at[sem],
            device_id=(gx - 1, gy - g), device_id_type=MESH,
        )

    def ahead(source, target, sem, g):
        return pltpu.make_async_remote_copy(
            src_ref=source, dst_ref=target, send_sem=send_sem.at[sem], recv_sem=recv_sem.at[sem],
            device_id=(gx + 1, gy + g), device_id_type=MESH,
        )

    def flag_copy(g):
        return back(flag_out, flag_in.at[g + 1], g + 1, g)

    def low_copy(n, g):
        return back(layers.at[n, pl.ds(0, 96)], low_in.at[n, g + 1], 3 + 3 * n + g + 1, g)

    def force_copy(n, g):
        return ahead(sums.at[n, g + 1], force_in.at[n, g + 1], 12 + 3 * n + g + 1, g)

    def send_back(copy):
        for side, ok in order:

            @pl.when(jnp.logical_and(back_ok, ok))
            def _():
                copy(-side).start()

    def got_back(copy):
        for g in (-1, 0, 1):

            @pl.when(jnp.logical_and(ahead_ok, side_ok[g]))
            def _():
                copy(g).wait_recv()

    def send_ahead(copy):
        for side, ok in order:

            @pl.when(jnp.logical_and(ahead_ok, ok))
            def _():
                copy(side).start()

    def got_ahead(copy):
        for g in (-1, 0, 1):

            @pl.when(jnp.logical_and(back_ok, side_ok[-g]))
            def _():
                copy(g).wait_recv()

    def is_pml(shape):
        return jnp.full(shape, flags[0], jnp.int32) > 0

    listed.wait()
    head.wait()
    big_row = lax.broadcasted_iota(jnp.int32, (128, 128), 0)
    big_col = lax.broadcasted_iota(jnp.int32, (128, 128), 1)
    same = (big_row >> 6) == (big_col >> 6)
    eye = jnp.where(big_row == big_col, 1.0, 0.0).astype(F32)
    own = is_pml((128, 128))
    basis_c, basis_ct, basis_p, basis_pt = (
        misc[ROW_C + i * 128 : ROW_C + (i + 1) * 128, :] for i in range(4)
    )
    ours, ours_t, ours_p, ours_pt = (
        jnp.where(own, eye, m) for m in (basis_c, basis_ct, basis_p, basis_pt)
    )
    q_row, q_col = big_row & 63, big_col & 63
    j_row = 2 * (q_row & 31) + (q_row >> 5)
    j_col = 2 * (q_col & 31) + (q_col >> 5)
    upper = big_row < 64
    step_one = jnp.where(
        upper,
        jnp.full((128, 128), faces[0, 3], jnp.int32),
        jnp.full((128, 128), faces[1, 3], jnp.int32),
    )

    def one_hot(where):
        return jnp.where(where, 1.0, 0.0).astype(BF16)

    def by_exact(a, b):
        hi, lo = split(a)
        return dot(jnp.concatenate([hi, lo], axis=1), jnp.concatenate([b, b], axis=0))

    def exact_by(a, b):
        hi, lo = split(b)
        return dot(jnp.concatenate([a, a], axis=1), jnp.concatenate([hi, lo], axis=0))

    one_pml = by_exact(ours_p, one_hot(jnp.logical_and(same, j_col == j_row - step_one)))
    one_air = dot(stacked(one_pml), right_form(basis_pt))
    two_pml, two_air = [], []
    for r in range(2):
        step_two = jnp.full((128, 128), faces[r, 4], jnp.int32)
        two_pml.append(exact_by(one_hot(jnp.logical_and(same, q_row == q_col - step_two)), ours_t))
        two_air.append(dot(stacked(basis_c), right_form(two_pml[r])))

    left[1] = left_form(one_pml.T)
    right[2] = right_form(two_pml[0].T)
    right[3] = right_form(two_pml[1].T)

    sides = 1 + (gy > 0).astype(jnp.int32) + (gy < ny - 1).astype(jnp.int32)
    ends = (gx > 0).astype(jnp.int32) + (gx < nx - 1).astype(jnp.int32)
    pl.semaphore_wait(barrier, sides * ends)
    send_back(flag_copy)

    def note_faces(partial, top, bottom, c):
        for d in range(3):
            acc[pl.ds(d * 256 + c, 8, stride=PLANE), :] = partial[d]
        picked[pl.ds(c, 8, stride=PLANE), :] = top
        picked[pl.ds(256 + c, 8, stride=PLANE), :] = bottom

    def face_part(partial, chunk_rows, r):
        tiles = chunk_rows.reshape(4, 8, 128)
        out = []
        for d in range(3):
            at = ROW_FACE + d * 128 + 32 * r
            weights = misc[at : at + 32, :].reshape(4, 8, 128)
            term = jnp.sum(weights * tiles, axis=0)
            out.append(term if partial is None else partial[d] + term)
        return out

    def gathered_faces():
        low, high = [], []
        pml = is_pml((PLANE, 128))
        for d in range(3):
            part = [acc[d * 256 + s * 32 : d * 256 + (s + 1) * 32, :] for s in range(8)]
            even = (part[0] + part[2]) + (part[4] + part[6])
            odd = (part[1] + part[3]) + (part[5] + part[7])
            row_low = picked[d * 32 : (d + 1) * 32, :]
            row_high = picked[256 + (7 - d) * 32 : 256 + (8 - d) * 32, :]
            low.append(jnp.where(pml, row_low, even + odd))
            high.append(jnp.where(pml, row_high, even - odd))
        return low + high

    for i in range(4):
        nows[i].wait()

        @pl.loop(0, TILES // 8)
        def _(t):
            window = state.at[0, :, pl.ds(pl.multiple_of(128 + i * chunk + t * 256, 128), 256)]
            for h in range(2):
                at = slice(h * 128, (h + 1) * 128)
                partial = None
                for r in range(4):
                    partial = face_part(partial, window[32 * r : 32 * r + 32, at], r)
                note_faces(partial, window[0:8, at], window[120:128, at], 8 * i + 2 * t + h)

    for e, plane in enumerate(gathered_faces()):
        layers[0, e * 32 : (e + 1) * 32, :] = plane
    send_back(lambda g: low_copy(0, g))

    def chosen(r, g):
        return jnp.logical_and(
            jnp.full((96, 128), faces[r, 2], jnp.int32) == g,
            jnp.full((96, 128), faces[r, 5], jnp.int32) > 0,
        )

    def make_sums(n):
        z = couple([layers[n, (3 + d) * 32 : (4 + d) * 32, :] for d in range(3)])
        z3 = stacked(jnp.concatenate(z, axis=0))
        product = dot(left[1], columns(dot(z3, right[2]), dot(z3, right[3])))
        moved = [jnp.concatenate(planes_of(product, r), axis=0) for r in range(2)]
        for g in (-1, 0, 1):
            total = jnp.where(chosen(0, g), moved[0], 0.0) + jnp.where(chosen(1, g), moved[1], 0.0)
            sums[n, g + 1] = total

    def high_force(n):
        parts = []
        for r in range(2):
            pick = jnp.zeros((96, 128), F32)
            for g in (-1, 0, 1):
                pick = jnp.where(chosen(r, g), low_in[n, g + 1], pick)
            parts.append(dot(stacked(pick), right[r]))
        product = dot(left[0], columns(parts[0], parts[1]))
        a, b = planes_of(product, 0), planes_of(product, 1)
        return couple([x + y for x, y in zip(a, b)])

    def low_force(n):
        total = jnp.zeros((96, 128), F32)
        for g in (-1, 0, 1):
            there = jnp.logical_and(back_ok, side_ok[-g]).astype(jnp.int32)
            total += jnp.where(jnp.full((96, 128), there, jnp.int32) > 0, force_in[n, g + 1], 0.0)
        return total

    def response(force):
        pml = is_pml((PLANE, 128))
        low, high = [], []
        for d in range(3):
            near, far = 0.0, 0.0
            for e in range(3):
                i = PAIRS[(min(d, e), max(d, e))]
                p = misc[ROW_P + i * 32 : ROW_P + (i + 1) * 32, :]
                q = misc[ROW_P + 192 + i * 32 : ROW_P + 192 + (i + 1) * 32, :]
                near = near + (p * force[e] + q * force[3 + e])
                far = far + (q * force[e] + p * force[3 + e])
            low.append(jnp.where(pml, FACE_COEF[d] * force[d], near))
            high.append(jnp.where(pml, FACE_COEF[3 + d] * force[3 + d], far))
        return low + high

    make_sums(0)
    send_ahead(lambda g: force_copy(0, g))
    got_back(flag_copy)

    def theirs(r):
        g = jnp.full((8, 128), faces[r, 2], jnp.int32)
        value = jnp.where(g == -1, flag_in[0], jnp.where(g == 0, flag_in[1], flag_in[2]))
        return jnp.broadcast_to(value[0:1, :], (128, 128))

    their = [theirs(r) for r in range(2)]
    their_col = jnp.where(big_col < 64, their[0], their[1]) > 0.5
    cross_one = jnp.where(their_col, one_pml, one_air)
    left[0] = left_form(cross_one)
    left[1] = left_form(cross_one.T)
    for r in range(2):
        cross_two = jnp.where(their[r] > 0.5, two_pml[r], two_air[r])
        right[r] = right_form(cross_two)
        right[2 + r] = right_form(cross_two.T)
    left[2] = left_form(ours_p)
    right[4] = right_form(ours_t)

    k = big_row.astype(F32)
    rate = 0.5 * ((k + 0.5) * (1.0 / S0)) ** 2
    inverse = 1.0 / (1.0 + rate)
    rows[0] = jnp.where(own, (1.0 - rate) * inverse, 1.0)
    rows[1] = jnp.where(own, (COURANT2 / 90.0) * inverse, 0.0)
    center = (2.0 + COURANT2 * CENTER3) * inverse
    edge = jnp.zeros((S0, 128), F32)
    for b in range(2):
        state[b, :, 0:128] = edge
        state[b, :, 128 + CROSS : 256 + CROSS] = edge
    for c in (0, 1, TILES + 2, TILES + 3):
        rolled[:, c * 128 : (c + 1) * 128] = edge
    pack[192:704, :] = jnp.zeros((512, 128), F32)
    rest[0].wait()

    def tile(c):
        return pl.ds(pl.multiple_of(c * 128, 128), 128)

    @pl.loop(0, TILES)
    def _(c):
        col = c * 128 + big_col
        mode_a = (col >> 6).astype(F32) * (math.pi / S1)
        mode_b = (col & 63).astype(F32) * (math.pi / S2)
        mode_k = k * (math.pi / S0)
        table = gain[:, tile(c)]
        doubled = 2.0 - table * (mode_k * mode_k + mode_a * mode_a + mode_b * mode_b)
        gain[:, tile(c)] = jnp.where(own, 0.0, table)
        slow[:, tile(c)] = jnp.where(own, center, doubled)

    rest[1].wait()
    rest[2].wait()

    alternate = (lax.broadcasted_iota(jnp.int32, (8, 128), 0) & 1) == 0

    def keep_force(force):
        pml = is_pml((PLANE, 128))
        for d in range(3):
            pack[d * 32 : (d + 1) * 32, :] = force[d] + force[3 + d]
            pack[96 + d * 32 : 96 + (d + 1) * 32, :] = force[d] - force[3 + d]
            pack[192 + d * 32 : 192 + (d + 1) * 32, :] = jnp.where(pml, FACE_COEF[d] * force[d], 0.0)
            at = 448 + (7 - d) * 32
            pack[at : at + 32, :] = jnp.where(pml, FACE_COEF[3 + d] * force[3 + d], 0.0)

    def finish(box, table, cut, turn, at, c0, n):
        for h in range(2):
            c = c0 + h
            here = slice(at + h * 128, at + (h + 1) * 128)
            box_here = slice(at + 128 + h * 128, at + 256 + h * 128)
            turn_here = slice(at + 256 + h * 128, at + 384 + h * 128)
            if n > 0:
                mode = mode_rows(pack, alternate, c)
                top = pack[pl.ds(192 + c, 8, stride=PLANE), :]
                bottom = pack[pl.ds(448 + c, 8, stride=PLANE), :]
            for r in range(4):
                row = slice(32 * r, 32 * r + 32)
                block = box[row, box_here]
                if n > 0:
                    block = block + table[row, here] * spread_modes(misc, mode, r)
                    if r == 0:
                        block = jnp.concatenate([block[0:8] + top, block[8:32]], axis=0)
                    if r == 3:
                        block = jnp.concatenate([block[0:24], block[24:32] + bottom], axis=0)
                    box[row, box_here] = block
                hi, lo = split(block)
                cut[row, here] = hi
                cut[slice(128 + 32 * r, 160 + 32 * r), here] = lo
                turn[row, turn_here] = pltpu.roll(block, 64, 1)

    w1, w2 = TAPS_90[0], TAPS_90[1]
    small_first = lax.broadcasted_iota(jnp.int32, (32, 128), 1) < 64

    def advance(b, p, n):
        def step(t, base, with_finish):
            width = 1024 if with_finish else 768
            box = state.at[b, :, pl.ds(base, 896 if with_finish else 512)]
            old = state.at[p, :, pl.ds(base, 512)]
            turn = rolled.at[:, pl.ds(base, width)]
            cut = halved.at[:, pl.ds(base, 768 if with_finish else 256)]
            pair = cut[:, 0:256]
            operand = jnp.concatenate([stencil[0:128, :], pair[0:128, :], pair[128:256, :]], axis=1)
            fixed = stencil[128:384, :]
            taps = dot(operand, jnp.concatenate([pair, fixed, fixed], axis=0))
            if with_finish:
                table = gain.at[:, pl.ds(base, 768)]
                finish(box, table, cut, turn, 512, 2 * t + 4, n)
            own_slow = slow.at[:, pl.ds(base, 256)]
            partial = [None, None]
            ends_ = [[None, None], [None, None]]
            for r in range(4):
                row = slice(32 * r, 32 * r + 32)
                ring = [turn[row, i * 128 : (i + 1) * 128] for i in range(6)]
                line = [box[row, i * 128 : (i + 1) * 128] for i in range(4)]
                quads = [w1 * (ring[i + 2] + ring[i + 1]) + (ring[i + 3] + ring[i]) for i in range(3)]
                for h in range(2):
                    at = slice(h * 128, (h + 1) * 128)
                    total = taps[row, at] + w2 * (line[h] + line[h + 2])
                    total += jnp.where(small_first, quads[h], quads[h + 1])
                    following = own_slow[row, at] * line[h + 1]
                    following -= rows[0, row, :] * old[row, 128 + h * 128 : 256 + h * 128]
                    following += rows[1, row, :] * total
                    old[row, 128 + h * 128 : 256 + h * 128] = following
                    partial[h] = face_part(partial[h], following, r)
                    if r == 0:
                        ends_[h][0] = following[0:8]
                    if r == 3:
                        ends_[h][1] = following[24:32]
            for h in range(2):
                note_faces(partial[h], ends_[h][0], ends_[h][1], 2 * t + h)

        for t in range(2):
            base = t * 256
            finish(
                state.at[b, :, pl.ds(base, 512)], gain.at[:, pl.ds(base, 256)], halved.at[:, pl.ds(base, 256)],
                rolled.at[:, pl.ds(base, 768)], 0, 2 * t, n,
            )

        @pl.loop(0, TILES // 2 - 2)
        def _(t):
            step(t, pl.multiple_of(t * 256, 256), True)

        for t in (TILES // 2 - 2, TILES // 2 - 1):
            step(t, t * 256, False)

        for e, plane in enumerate(gathered_faces()):
            free[e * 32 : (e + 1) * 32, :] = plane

    unforced = pltpu.make_async_copy(
        state.at[STEPS % 2, :, pl.ds(128, CROSS)], free_out, out_sem.at[0]
    )
    for n in range(STEPS):
        b, p = n % 2, 1 - n % 2
        if n > 0:
            send_back(lambda g: low_copy(n, g))
            make_sums(n)
            send_ahead(lambda g: force_copy(n, g))
        advance(b, p, n)
        if n == STEPS - 1:
            unforced.start()
        got_back(lambda g: low_copy(n, g))
        high = high_force(n)
        got_ahead(lambda g: force_copy(n, g))
        low = low_force(n)
        if n == 0:
            turned = dot(stacked(low), right[4])
            low = planes_of(dot(left[2], columns(turned, jnp.zeros((96, 128), F32))), 0)
        else:
            low = [low[e * 32 : (e + 1) * 32, :] for e in range(3)]
        force = low + high
        for e, plane in enumerate(response(force)):
            at = slice(e * 32, (e + 1) * 32)
            layers[n + 1, at, :] = free[at, :] + plane
        keep_force(force)

    pack[704:896, :] = layers[STEPS]
    packed = pltpu.make_async_copy(pack, pack_out, out_sem.at[1])
    packed.start()

    for side, ok in order:

        @pl.when(jnp.logical_and(back_ok, ok))
        def _():
            flag_copy(-side).wait_send()
            for n in range(STEPS):
                low_copy(n, -side).wait_send()

        @pl.when(jnp.logical_and(ahead_ok, ok))
        def _():
            for n in range(STEPS):
                force_copy(n, side).wait_send()

    unforced.wait()
    packed.wait()


def mode_rows(pack, alternate, c):
    out = []
    for d in range(3):
        plus = jnp.broadcast_to(pack[pl.ds(d * 32 + c, 1), :], (8, 128))
        minus = jnp.broadcast_to(pack[pl.ds(96 + d * 32 + c, 1), :], (8, 128))
        out.append(jnp.where(alternate, plus, minus))
    return out


def spread_modes(table, mode, r):
    total = None
    for d in range(3):
        at = ROW_FACE + d * 128 + 32 * r
        term = table[at : at + 32, :].reshape(4, 8, 128) * mode[d][None]
        total = term if total is None else total + term
    return total.reshape(32, 128)


PARTS = 8
WIDE = CROSS // PARTS


def close(flags, pack, misc, free, gain, out, layers_out, done, sems):
    pml = flags[0] > 0
    leave = [
        pltpu.make_async_copy(
            done.at[:, pl.ds(i * WIDE, WIDE)], out.at[0, :, pl.ds(i * WIDE, WIDE)], sems.at[i]
        )
        for i in range(PARTS)
    ]

    @pl.when(pml)
    def _():
        for i in range(PARTS):
            at = slice(i * WIDE, (i + 1) * WIDE)
            done[:, at] = free[:, at]
            for h in range(WIDE // 128):
                c = i * (WIDE // 128) + h
                at = slice(c * 128, (c + 1) * 128)
                done[0:8, at] = free[0:8, at] + pack[pl.ds(192 + c, 8, stride=PLANE), :]
                done[120:128, at] = free[120:128, at] + pack[pl.ds(448 + c, 8, stride=PLANE), :]
            leave[i].start()
        layers_out[...] = pack[704:896, :]

    @pl.when(jnp.logical_not(pml))
    def _():
        alternate = (lax.broadcasted_iota(jnp.int32, (8, 128), 0) & 1) == 0
        for i in range(PARTS):

            @pl.loop(0, WIDE // 256)
            def _(t):
                window = pl.ds(pl.multiple_of(i * WIDE + t * 256, 256), 256)
                source, table, target = free.at[:, window], gain.at[:, window], done.at[:, window]
                for h in range(2):
                    at = slice(h * 128, (h + 1) * 128)
                    mode = mode_rows(pack, alternate, i * (WIDE // 128) + 2 * t + h)
                    for r in range(4):
                        row = slice(32 * r, 32 * r + 32)
                        target[row, at] = source[row, at] + table[row, at] * spread_modes(misc, mode, r)

            leave[i].start()
        turned = dot(stacked(pack[704:896, :]), right_form(misc[ROW_C : ROW_C + 128, :]))
        ours_pt = left_form(misc[ROW_C + 384 : ROW_C + 512, :])
        product = dot(ours_pt, columns(turned[0:96, :], turned[96:192, :]))
        for s in range(2):
            for e, plane in enumerate(planes_of(product, s)):
                at = (3 * s + e) * 32
                layers_out[at : at + 32, :] = plane

    for copy in leave:
        copy.wait()


def local(state_now, state_prev, pml_flags, interfaces):
    gain, misc, stencil = (jnp.asarray(a) for a in constants())
    smem = pl.BlockSpec(memory_space=pltpu.SMEM)
    hbm = pl.BlockSpec(memory_space=pltpu.HBM)
    free, pack = pl.pallas_call(
        exchange,
        out_shape=(
            jax.ShapeDtypeStruct((S0, CROSS), F32),
            jax.ShapeDtypeStruct((896, 128), F32),
        ),
        in_specs=[smem, hbm, hbm, hbm, hbm, hbm, hbm],
        out_specs=(pl.BlockSpec(memory_space=pl.ANY),) * 2,
        scratch_shapes=[
            pltpu.VMEM((2, S0, CROSS + 256), F32),
            pltpu.VMEM((S0, CROSS), F32),
            pltpu.VMEM((S0, CROSS), F32),
            pltpu.VMEM(misc.shape, F32),
            pltpu.VMEM(stencil.shape, BF16),
            pltpu.VMEM((256, CROSS), BF16),
            pltpu.VMEM((S0, CROSS + 512), F32),
            pltpu.VMEM((2, 128, 128), F32),
            pltpu.VMEM((768, 128), F32),
            pltpu.VMEM((512, 128), F32),
            pltpu.VMEM((192, 128), F32),
            pltpu.VMEM((3, 128, 384), BF16),
            pltpu.VMEM((5, 384, 128), BF16),
            pltpu.VMEM((8, 128), F32),
            pltpu.VMEM((3, 8, 128), F32),
            pltpu.VMEM((STEPS + 1, 192, 128), F32),
            pltpu.VMEM((STEPS, 3, 96, 128), F32),
            pltpu.VMEM((STEPS, 3, 96, 128), F32),
            pltpu.VMEM((STEPS, 3, 96, 128), F32),
            pltpu.VMEM((896, 128), F32),
            pltpu.SMEM((2, 6), jnp.int32),
            pltpu.SemaphoreType.DMA((9,)),
            pltpu.SemaphoreType.DMA((21,)),
            pltpu.SemaphoreType.DMA((21,)),
            pltpu.SemaphoreType.DMA((2,)),
        ],
        compiler_params=pltpu.CompilerParams(
            collective_id=0, has_side_effects=True, vmem_limit_bytes=32 * 1024 * 1024
        ),
    )(
        pml_flags,
        *(
            pltpu.with_memory_space_constraint(x, pltpu.HBM)
            for x in (interfaces, state_now, state_prev, gain, misc, stencil)
        ),
    )

    whole = pl.BlockSpec(memory_space=pltpu.VMEM)
    new_state, planes = pl.pallas_call(
        close,
        out_shape=(
            jax.ShapeDtypeStruct((1, S0, CROSS), F32),
            jax.ShapeDtypeStruct((192, 128), F32),
        ),
        in_specs=[smem, whole, whole, whole, whole],
        out_specs=(hbm, whole),
        scratch_shapes=[pltpu.VMEM((S0, CROSS), F32), pltpu.SemaphoreType.DMA((PARTS,))],
        compiler_params=pltpu.CompilerParams(vmem_limit_bytes=24 * 1024 * 1024),
    )(pml_flags, pack, misc, free, gain)
    return new_state, planes.reshape(1, 6, CROSS)


def solution(mesh):
    one, two, three = P(("gx", "gy")), P(("gx", "gy"), None), P(("gx", "gy"), None, None)
    return jax.shard_map(
        local,
        mesh=mesh,
        in_specs=(three, three, one, two),
        out_specs=(three, three),
        check_vma=False,
    )
```

```python
import math

import jax
import jax.numpy as jnp
import numpy as np
from jax import lax
from jax.experimental import pallas as pl
from jax.experimental.pallas import tpu as pltpu
from jax.sharding import PartitionSpec as P

S0 = 128
S1 = 64
S2 = 64
CROSS = S1 * S2
STEPS = 3
TILES = CROSS // 128
PLANE = 32
MESH = pl.DeviceIdType.MESH
F32 = jnp.float32
BF16 = jnp.bfloat16

COURANT2 = 0.16
CENTER3 = 3.0 * (-490.0 / 180.0)
TAPS = (1.5, -0.15, 1.0 / 90.0)
TAPS_90 = (135.0, -13.5, 1.0)
PAIRS = {(0, 0): 0, (0, 1): 1, (0, 2): 2, (1, 1): 3, (1, 2): 4, (2, 2): 5}


def basis(n):
    k = np.arange(n)[:, None]
    i = np.arange(n)[None, :]
    weight = np.where(k == 0, math.sqrt(1.0 / n), math.sqrt(2.0 / n))
    return weight * np.cos(math.pi * k * (i + 0.5) / n)


def twice(a):
    n = a.shape[0]
    out = np.zeros((2 * n, 2 * n))
    out[:n, :n] = a
    out[n:, n:] = a
    return out


def constants():
    c0, c1 = basis(S0), basis(S1)
    k = (math.pi * np.arange(S0) / S0) ** 2
    a = (math.pi * np.arange(S1) / S1) ** 2
    wave = (k[:, None, None] + a[None, :, None] + a[None, None, :]).reshape(S0, CROSS)
    safe = np.where(wave > 0, wave, 1.0)
    gain = np.where(wave > 0, 4.0 * np.sin(0.2 * np.sqrt(wave)) ** 2 / safe, COURANT2)
    face = c0[:, :3]
    sign = (-1.0) ** np.arange(S0)
    planes = []
    for s in (np.ones(S0), sign):
        for d, e in PAIRS:
            planes.append(((face[:, d] * face[:, e] * s) @ gain).reshape(PLANE, 128))
    order = np.concatenate([np.arange(0, S1, 2), np.arange(1, S1, 2)])
    c1p = c1[order][:, order]
    misc = np.concatenate(
        [np.repeat(face[:, d : d + 1], 128, axis=1) for d in range(3)]
        + planes
        + [twice(c1), twice(c1.T), twice(c1p), twice(c1p.T)],
        axis=0,
    )

    def band(n):
        out = np.zeros((n, n))
        for distance, tap in enumerate(TAPS_90, 1):
            out += tap * (np.eye(n, k=distance) + np.eye(n, k=-distance))
        return out

    along = band(S0)
    stencil = np.concatenate([np.concatenate([along, along], axis=1), twice(twice(band(S2)))], axis=0)
    six = np.zeros((S0, 8))
    six[:, 0:6] = c0[:, [0, 1, 2, 127, 126, 125]]
    high = six.astype(np.float32).astype(BF16)
    low = (six - high.astype(np.float64)).astype(np.float32).astype(BF16)
    modes = np.concatenate([high, high, low, np.zeros((S0, 8), BF16)], axis=1)
    return gain.astype(np.float32), misc.astype(np.float32), stencil.astype(BF16), modes


ROW_FACE, ROW_P, ROW_C = 0, 384, 768


def rate_of(row):
    return 0.5 * ((row + 0.5) / S0) ** 2


FACE_COEF = [COURANT2 / (1.0 + rate_of(i)) for i in (0, 1, 2, 127, 126, 125)]


def split(x):
    high = x.astype(BF16)
    return high, (x - high.astype(F32)).astype(BF16)


def dot(a, b):
    return jnp.dot(a, b, preferred_element_type=F32)


def couple(p):
    w1, w2, w3 = TAPS
    return [w1 * p[0] + w2 * p[1] + w3 * p[2], w2 * p[0] + w3 * p[1], w3 * p[0]]


def stacked(x):
    hi, lo = split(x)
    return jnp.concatenate([hi, lo, hi], axis=1)


def first_half():
    return lax.broadcasted_iota(jnp.int32, (PLANE, 128), 1) < 64


def columns(*sets):
    first = first_half()
    outer = []
    for w in sets:
        even, odd = [], []
        for e in range(3):
            p = w[e * 32 : (e + 1) * 32, :]
            swapped = pltpu.roll(p, 64, 1)
            even.append(jnp.where(first, p, swapped))
            odd.append(jnp.where(first, swapped, p))
        outer.append(jnp.concatenate(even, axis=1))
        outer.append(jnp.concatenate(odd, axis=1))
    hi, lo = split(jnp.concatenate(outer, axis=0))
    return jnp.concatenate([hi, lo, hi], axis=0)


def planes_of(product, s):
    first = first_half()
    top = product[64 * s : 64 * s + 32, :]
    bottom = product[64 * s + 32 : 64 * s + 64, :]
    return [
        jnp.where(first, top[:, e * 128 : (e + 1) * 128], bottom[:, e * 128 : (e + 1) * 128])
        for e in range(3)
    ]


def left_form(matrix):
    hi, lo = split(matrix)
    return jnp.concatenate([hi, hi, lo], axis=1)


def right_form(matrix):
    hi, lo = split(matrix)
    return jnp.concatenate([hi, hi, lo], axis=0)


def exchange(
    flags, faces_hbm, now_hbm, prev_hbm, gain_hbm, misc_hbm, stencil_hbm, modes_hbm,
    free_out, pack_out,
    state, gain, slow, misc, modes, stencil, halved, rolled, tapped, rows,
    acc, picked, free, left, right, flag_out, flag_in, layers, sums, low_in, force_in, pack,
    faces, load_sem, send_sem, recv_sem, out_sem,
):
    gx, gy = lax.axis_index("gx"), lax.axis_index("gy")
    nx, ny = lax.axis_size("gx"), lax.axis_size("gy")

    back_ok, ahead_ok = gx > 0, gx < nx - 1
    side_ok = {-1: gy > 0, 0: gy >= 0, 1: gy < ny - 1}
    barrier = pltpu.get_barrier_semaphore()
    for ok, to_x in ((back_ok, gx - 1), (ahead_ok, gx + 1)):
        for side in (-1, 0, 1):

            @pl.when(jnp.logical_and(ok, side_ok[side]))
            def _():
                pl.semaphore_signal(barrier, inc=1, device_id=(to_x, gy + side), device_id_type=MESH)

    head = pltpu.make_async_copy(misc_hbm, misc, load_sem.at[0])
    head.start()
    listed = pltpu.make_async_copy(faces_hbm, faces, load_sem.at[8])
    listed.start()
    chunk = CROSS // 4
    nows = [
        pltpu.make_async_copy(
            now_hbm.at[0, :, pl.ds(i * chunk, chunk)],
            state.at[0, :, pl.ds(128 + i * chunk, chunk)],
            load_sem.at[4 + i],
        )
        for i in range(4)
    ]
    for load in nows:
        load.start()
    rest = [
        pltpu.make_async_copy(gain_hbm, gain, load_sem.at[1]),
        pltpu.make_async_copy(prev_hbm.at[0], state.at[1, :, pl.ds(128, CROSS)], load_sem.at[2]),
        pltpu.make_async_copy(stencil_hbm, stencil, load_sem.at[3]),
        pltpu.make_async_copy(modes_hbm, modes, load_sem.at[9]),
    ]
    for load in rest:
        load.start()
    flag_out[...] = jnp.full(flag_out.shape, flags[0], jnp.int32).astype(F32)

    core = lax.rem(gy, 2)
    away = 2 * core - 1
    away_ok = jnp.where(core == 0, gy > 0, gy < ny - 1)
    order = ((away, away_ok), (-away, gy >= 0), (0, gy >= 0))

    def back(source, target, sem, g):
        return pltpu.make_async_remote_copy(
            src_ref=source, dst_ref=target, send_sem=send_sem.at[sem], recv_sem=recv_sem.at[sem],
            device_id=(gx - 1, gy - g), device_id_type=MESH,
        )

    def ahead(source, target, sem, g):
        return pltpu.make_async_remote_copy(
            src_ref=source, dst_ref=target, send_sem=send_sem.at[sem], recv_sem=recv_sem.at[sem],
            device_id=(gx + 1, gy + g), device_id_type=MESH,
        )

    def flag_copy(g):
        return back(flag_out, flag_in.at[g + 1], g + 1, g)

    def low_copy(n, g):
        return back(layers.at[n, pl.ds(0, 96)], low_in.at[n, g + 1], 3 + 3 * n + g + 1, g)

    def force_copy(n, g):
        return ahead(sums.at[n, g + 1], force_in.at[n, g + 1], 12 + 3 * n + g + 1, g)

    def send_back(copy):
        for side, ok in order:

            @pl.when(jnp.logical_and(back_ok, ok))
            def _():
                copy(-side).start()

    def got_back(copy):
        for g in (-1, 0, 1):

            @pl.when(jnp.logical_and(ahead_ok, side_ok[g]))
            def _():
                copy(g).wait_recv()

    def send_ahead(copy):
        for side, ok in order:

            @pl.when(jnp.logical_and(ahead_ok, ok))
            def _():
                copy(side).start()

    def got_ahead(copy):
        for g in (-1, 0, 1):

            @pl.when(jnp.logical_and(back_ok, side_ok[-g]))
            def _():
                copy(g).wait_recv()

    def is_pml(shape):
        return jnp.full(shape, flags[0], jnp.int32) > 0

    listed.wait()
    head.wait()
    big_row = lax.broadcasted_iota(jnp.int32, (128, 128), 0)
    big_col = lax.broadcasted_iota(jnp.int32, (128, 128), 1)
    same = (big_row >> 6) == (big_col >> 6)
    eye = jnp.where(big_row == big_col, 1.0, 0.0).astype(F32)
    own = is_pml((128, 128))
    basis_c, basis_ct, basis_p, basis_pt = (
        misc[ROW_C + i * 128 : ROW_C + (i + 1) * 128, :] for i in range(4)
    )
    ours, ours_t, ours_p, ours_pt = (
        jnp.where(own, eye, m) for m in (basis_c, basis_ct, basis_p, basis_pt)
    )
    q_row, q_col = big_row & 63, big_col & 63
    j_row = 2 * (q_row & 31) + (q_row >> 5)
    j_col = 2 * (q_col & 31) + (q_col >> 5)
    upper = big_row < 64
    step_one = jnp.where(
        upper,
        jnp.full((128, 128), faces[0, 3], jnp.int32),
        jnp.full((128, 128), faces[1, 3], jnp.int32),
    )

    def one_hot(where):
        return jnp.where(where, 1.0, 0.0).astype(BF16)

    def by_exact(a, b):
        hi, lo = split(a)
        return dot(jnp.concatenate([hi, lo], axis=1), jnp.concatenate([b, b], axis=0))

    def exact_by(a, b):
        hi, lo = split(b)
        return dot(jnp.concatenate([a, a], axis=1), jnp.concatenate([hi, lo], axis=0))

    one_pml = by_exact(ours_p, one_hot(jnp.logical_and(same, j_col == j_row - step_one)))
    one_air = dot(stacked(one_pml), right_form(basis_pt))
    two_pml, two_air = [], []
    for r in range(2):
        step_two = jnp.full((128, 128), faces[r, 4], jnp.int32)
        two_pml.append(exact_by(one_hot(jnp.logical_and(same, q_row == q_col - step_two)), ours_t))
        two_air.append(dot(stacked(basis_c), right_form(two_pml[r])))

    left[1] = left_form(one_pml.T)
    right[2] = right_form(two_pml[0].T)
    right[3] = right_form(two_pml[1].T)

    sides = 1 + (gy > 0).astype(jnp.int32) + (gy < ny - 1).astype(jnp.int32)
    ends = (gx > 0).astype(jnp.int32) + (gx < nx - 1).astype(jnp.int32)
    pl.semaphore_wait(barrier, sides * ends)
    send_back(flag_copy)

    def note_faces(partial, top, bottom, c):
        for d in range(3):
            acc[pl.ds(d * 256 + c, 8, stride=PLANE), :] = partial[d]
        picked[pl.ds(c, 8, stride=PLANE), :] = top
        picked[pl.ds(256 + c, 8, stride=PLANE), :] = bottom

    def face_part(partial, chunk_rows, r):
        tiles = chunk_rows.reshape(4, 8, 128)
        out = []
        for d in range(3):
            at = ROW_FACE + d * 128 + 32 * r
            weights = misc[at : at + 32, :].reshape(4, 8, 128)
            term = jnp.sum(weights * tiles, axis=0)
            out.append(term if partial is None else partial[d] + term)
        return out

    def gathered_faces():
        low, high = [], []
        pml = is_pml((PLANE, 128))
        for d in range(3):
            part = [acc[d * 256 + s * 32 : d * 256 + (s + 1) * 32, :] for s in range(8)]
            even = (part[0] + part[2]) + (part[4] + part[6])
            odd = (part[1] + part[3]) + (part[5] + part[7])
            row_low = picked[d * 32 : (d + 1) * 32, :]
            row_high = picked[256 + (7 - d) * 32 : 256 + (8 - d) * 32, :]
            low.append(jnp.where(pml, row_low, even + odd))
            high.append(jnp.where(pml, row_high, even - odd))
        return low + high

    for i in range(4):
        nows[i].wait()

        @pl.loop(0, TILES // 8)
        def _(t):
            window = state.at[0, :, pl.ds(pl.multiple_of(128 + i * chunk + t * 256, 128), 256)]
            for h in range(2):
                at = slice(h * 128, (h + 1) * 128)
                partial = None
                for r in range(4):
                    partial = face_part(partial, window[32 * r : 32 * r + 32, at], r)
                note_faces(partial, window[0:8, at], window[120:128, at], 8 * i + 2 * t + h)

    for e, plane in enumerate(gathered_faces()):
        layers[0, e * 32 : (e + 1) * 32, :] = plane
    send_back(lambda g: low_copy(0, g))

    def chosen(r, g):
        return jnp.logical_and(
            jnp.full((96, 128), faces[r, 2], jnp.int32) == g,
            jnp.full((96, 128), faces[r, 5], jnp.int32) > 0,
        )

    def make_sums(n):
        z = couple([layers[n, (3 + d) * 32 : (4 + d) * 32, :] for d in range(3)])
        z3 = stacked(jnp.concatenate(z, axis=0))
        product = dot(left[1], columns(dot(z3, right[2]), dot(z3, right[3])))
        moved = [jnp.concatenate(planes_of(product, r), axis=0) for r in range(2)]
        for g in (-1, 0, 1):
            total = jnp.where(chosen(0, g), moved[0], 0.0) + jnp.where(chosen(1, g), moved[1], 0.0)
            sums[n, g + 1] = total

    def high_force(n):
        parts = []
        for r in range(2):
            pick = jnp.zeros((96, 128), F32)
            for g in (-1, 0, 1):
                pick = jnp.where(chosen(r, g), low_in[n, g + 1], pick)
            parts.append(dot(stacked(pick), right[r]))
        product = dot(left[0], columns(parts[0], parts[1]))
        a, b = planes_of(product, 0), planes_of(product, 1)
        return couple([x + y for x, y in zip(a, b)])

    def low_force(n):
        total = jnp.zeros((96, 128), F32)
        for g in (-1, 0, 1):
            there = jnp.logical_and(back_ok, side_ok[-g]).astype(jnp.int32)
            total += jnp.where(jnp.full((96, 128), there, jnp.int32) > 0, force_in[n, g + 1], 0.0)
        return total

    def response(force):
        pml = is_pml((PLANE, 128))
        low, high = [], []
        for d in range(3):
            near, far = 0.0, 0.0
            for e in range(3):
                i = PAIRS[(min(d, e), max(d, e))]
                p = misc[ROW_P + i * 32 : ROW_P + (i + 1) * 32, :]
                q = misc[ROW_P + 192 + i * 32 : ROW_P + 192 + (i + 1) * 32, :]
                near = near + (p * force[e] + q * force[3 + e])
                far = far + (q * force[e] + p * force[3 + e])
            low.append(jnp.where(pml, FACE_COEF[d] * force[d], near))
            high.append(jnp.where(pml, FACE_COEF[3 + d] * force[3 + d], far))
        return low + high

    make_sums(0)
    send_ahead(lambda g: force_copy(0, g))
    k = big_row.astype(F32)
    rate = 0.5 * ((k + 0.5) * (1.0 / S0)) ** 2
    inverse = 1.0 / (1.0 + rate)
    rows[0] = jnp.where(own, (1.0 - rate) * inverse, 1.0)
    rows[1] = jnp.where(own, (COURANT2 / 90.0) * inverse, 0.0)
    center = (2.0 + COURANT2 * CENTER3) * inverse
    mode_k = (k * (math.pi / S0)) * (k * (math.pi / S0))
    edge = jnp.zeros((S0, 128), F32)
    for b in range(2):
        state[b, :, 0:128] = edge
        state[b, :, 128 + CROSS : 256 + CROSS] = edge
    for c in (0, 1, TILES + 2, TILES + 3):
        rolled[:, c * 128 : (c + 1) * 128] = edge
    pack[192:768, :] = jnp.zeros((576, 128), F32)
    rest[0].wait()

    def tile(c):
        return pl.ds(pl.multiple_of(c * 128, 128), 128)

    @pl.loop(0, TILES)
    def _(c):
        col = c * 128 + lax.broadcasted_iota(jnp.int32, (1, 128), 1)
        mode_a = (col >> 6).astype(F32) * (math.pi / S1)
        mode_b = (col & 63).astype(F32) * (math.pi / S2)
        wave = mode_k + (mode_a * mode_a + mode_b * mode_b)
        slow[:, tile(c)] = jnp.where(own, center, 2.0 - gain[:, tile(c)] * wave)

    rest[1].wait()
    rest[2].wait()
    rest[3].wait()

    def keep_force(force):
        pml = is_pml((PLANE, 128))
        for d in range(3):
            pack[d * 32 : (d + 1) * 32, :] = jnp.where(pml, 0.0, force[d])
            pack[96 + d * 32 : 96 + (d + 1) * 32, :] = jnp.where(pml, 0.0, force[3 + d])
            pack[256 + d * 32 : 256 + (d + 1) * 32, :] = jnp.where(pml, FACE_COEF[d] * force[d], 0.0)
            at = 512 + (7 - d) * 32
            pack[at : at + 32, :] = jnp.where(pml, FACE_COEF[3 + d] * force[3 + d], 0.0)

    def finish(box, table, cut, turn, at, c0, n):
        if n > 0:
            along_box = spread_modes(modes, pack, c0)
            top = both(pack, 256, c0)
            bottom = both(pack, 512, c0)
        for r in range(4):
            row = slice(32 * r, 32 * r + 32)
            for h in range(2):
                here = slice(at + h * 128, at + (h + 1) * 128)
                box_here = slice(at + 128 + h * 128, at + 256 + h * 128)
                turn_here = slice(at + 256 + h * 128, at + 384 + h * 128)
                side = slice(h * 128, (h + 1) * 128)
                block = box[row, box_here]
                if n > 0:
                    block = block + table[row, here] * along_box[row, side]
                    if r == 0:
                        block = jnp.concatenate([block[0:8] + top[:, side], block[8:32]], axis=0)
                    if r == 3:
                        block = jnp.concatenate([block[0:24], block[24:32] + bottom[:, side]], axis=0)
                    box[row, box_here] = block
                hi, lo = split(block)
                cut[row, here] = hi
                cut[slice(128 + 32 * r, 160 + 32 * r), here] = lo
                turn[row, turn_here] = pltpu.roll(block, 64, 1)

    w1, w2 = TAPS_90[0], TAPS_90[1]
    small_first = lax.broadcasted_iota(jnp.int32, (32, 128), 1) < 64

    def keep_taps(cut, at, slot):
        pair = cut[:, at : at + 256]
        operand = jnp.concatenate([stencil[0:128, :], pair[0:128, :], pair[128:256, :]], axis=1)
        fixed = stencil[128:384, :]
        tapped[slot] = dot(operand, jnp.concatenate([pair, fixed, fixed], axis=0))

    def advance(b, p, n):
        def step(base, c0, at, slot, ahead_by, width):
            box = state.at[b, :, pl.ds(base, 256 + width)]
            old = state.at[p, :, pl.ds(base, 256 + width)]
            turn = rolled.at[:, pl.ds(base, 512 + width)]
            cut = halved.at[:, pl.ds(base, width)]
            table = gain.at[:, pl.ds(base, width)]
            own_slow = slow.at[:, pl.ds(base, width)]
            if ahead_by > 0:
                keep_taps(cut, at + 256, 1 - slot)
            if ahead_by > 1:
                finish(box, table, cut, turn, at + 512, c0 + 4, n)
            partial = [None, None]
            ends_ = [[None, None], [None, None]]
            for r in range(4):
                row = slice(32 * r, 32 * r + 32)
                ring = [turn[row, at + i * 128 : at + (i + 1) * 128] for i in range(6)]
                line = [box[row, at + i * 128 : at + (i + 1) * 128] for i in range(4)]
                quads = [w1 * (ring[i + 2] + ring[i + 1]) + (ring[i + 3] + ring[i]) for i in range(3)]
                for h in range(2):
                    here = slice(at + h * 128, at + (h + 1) * 128)
                    box_here = slice(at + 128 + h * 128, at + 256 + h * 128)
                    total = tapped[slot, row, h * 128 : (h + 1) * 128] + w2 * (line[h] + line[h + 2])
                    total += jnp.where(small_first, quads[h], quads[h + 1])
                    following = own_slow[row, here] * line[h + 1]
                    following -= rows[0, row, :] * old[row, box_here]
                    following += rows[1, row, :] * total
                    old[row, box_here] = following
                    partial[h] = face_part(partial[h], following, r)
                    if r == 0:
                        ends_[h][0] = following[0:8]
                    if r == 3:
                        ends_[h][1] = following[24:32]
            for h in range(2):
                note_faces(partial[h], ends_[h][0], ends_[h][1], c0 + h)

        for t in range(2):
            base = t * 256
            finish(
                state.at[b, :, pl.ds(base, 512)], gain.at[:, pl.ds(base, 256)], halved.at[:, pl.ds(base, 256)],
                rolled.at[:, pl.ds(base, 768)], 0, 2 * t, n,
            )
        keep_taps(halved, 0, 0)

        @pl.loop(0, TILES // 4 - 1)
        def _(i):
            base = pl.multiple_of(i * 512, 512)
            for s in range(2):
                step(base, 4 * i + 2 * s, 256 * s, s, 2, 1024)

        base = CROSS - 512
        step(base, TILES - 4, 0, 0, 1, 512)
        step(base, TILES - 2, 256, 1, 0, 512)

        for e, plane in enumerate(gathered_faces()):
            free[e * 32 : (e + 1) * 32, :] = plane

    def theirs(r):
        g = jnp.full((8, 128), faces[r, 2], jnp.int32)
        value = jnp.where(g == -1, flag_in[0], jnp.where(g == 0, flag_in[1], flag_in[2]))
        return jnp.broadcast_to(value[0:1, :], (128, 128))

    def finish_matrices():
        got_back(flag_copy)
        their = [theirs(r) for r in range(2)]
        their_col = jnp.where(big_col < 64, their[0], their[1]) > 0.5
        cross_one = jnp.where(their_col, one_pml, one_air)
        left[0] = left_form(cross_one)
        left[1] = left_form(cross_one.T)
        for r in range(2):
            cross_two = jnp.where(their[r] > 0.5, two_pml[r], two_air[r])
            right[r] = right_form(cross_two)
            right[2 + r] = right_form(cross_two.T)
        left[2] = left_form(ours_p)
        right[4] = right_form(ours_t)

    unforced = pltpu.make_async_copy(
        state.at[STEPS % 2, :, pl.ds(128, CROSS)], free_out, out_sem.at[0]
    )
    for n in range(STEPS):
        b, p = n % 2, 1 - n % 2
        if n > 0:
            send_back(lambda g: low_copy(n, g))
            make_sums(n)
            send_ahead(lambda g: force_copy(n, g))
            keep_force(force)
        advance(b, p, n)
        if n == 0:
            finish_matrices()
        if n == STEPS - 1:
            unforced.start()
        got_back(lambda g: low_copy(n, g))
        high = high_force(n)
        got_ahead(lambda g: force_copy(n, g))
        low = low_force(n)
        if n == 0:
            turned = dot(stacked(low), right[4])
            low = planes_of(dot(left[2], columns(turned, jnp.zeros((96, 128), F32))), 0)
        else:
            low = [low[e * 32 : (e + 1) * 32, :] for e in range(3)]
        force = low + high
        for e, plane in enumerate(response(force)):
            at = slice(e * 32, (e + 1) * 32)
            layers[n + 1, at, :] = free[at, :] + plane

    keep_force(force)
    pack[768:960, :] = layers[STEPS]
    packed = pltpu.make_async_copy(pack, pack_out, out_sem.at[1])
    packed.start()

    for side, ok in order:

        @pl.when(jnp.logical_and(back_ok, ok))
        def _():
            flag_copy(-side).wait_send()
            for n in range(STEPS):
                low_copy(n, -side).wait_send()

        @pl.when(jnp.logical_and(ahead_ok, ok))
        def _():
            for n in range(STEPS):
                force_copy(n, side).wait_send()

    unforced.wait()
    packed.wait()


def both(pack, row, c):
    return jnp.concatenate([pack[pl.ds(row + c + h, 8, stride=PLANE), :] for h in range(2)], axis=1)


def spread_modes(modes, pack, c):
    hi, lo = split(both(pack, 0, c))
    hi = hi.astype(F32)
    terms = jnp.concatenate([hi, lo.astype(F32), hi, jnp.zeros((8, 256), F32)], axis=0)
    return dot(modes[...], terms.astype(BF16))


PARTS = 8
WIDE = CROSS // PARTS


def close(flags, pack, misc, free, gain, out, layers_out, done, sems):
    pml = flags[0] > 0
    leave = [
        pltpu.make_async_copy(
            done.at[:, pl.ds(i * WIDE, WIDE)], out.at[0, :, pl.ds(i * WIDE, WIDE)], sems.at[i]
        )
        for i in range(PARTS)
    ]

    @pl.when(pml)
    def _():
        for i in range(PARTS):
            at = slice(i * WIDE, (i + 1) * WIDE)
            done[:, at] = free[:, at]
            for h in range(WIDE // 128):
                c = i * (WIDE // 128) + h
                at = slice(c * 128, (c + 1) * 128)
                done[0:8, at] = free[0:8, at] + pack[pl.ds(256 + c, 8, stride=PLANE), :]
                done[120:128, at] = free[120:128, at] + pack[pl.ds(512 + c, 8, stride=PLANE), :]
            leave[i].start()
        layers_out[...] = pack[768:960, :]

    @pl.when(jnp.logical_not(pml))
    def _():
        even = (lax.broadcasted_iota(jnp.int32, (8, 128), 0) & 1) == 0
        for i in range(PARTS):

            @pl.loop(0, WIDE // 256)
            def _(t):
                window = pl.ds(pl.multiple_of(i * WIDE + t * 256, 256), 256)
                source, table, target = free.at[:, window], gain.at[:, window], done.at[:, window]
                for h in range(2):
                    at = slice(h * 128, (h + 1) * 128)
                    c = i * (WIDE // 128) + 2 * t + h
                    mode = []
                    for d in range(3):
                        low = jnp.broadcast_to(pack[pl.ds(d * 32 + c, 1), :], (8, 128))
                        high = jnp.broadcast_to(pack[pl.ds(96 + d * 32 + c, 1), :], (8, 128))
                        mode.append(low + jnp.where(even, high, -high))
                    for r in range(4):
                        row = slice(32 * r, 32 * r + 32)
                        total = None
                        for d in range(3):
                            at_d = ROW_FACE + d * 128 + 32 * r
                            term = misc[at_d : at_d + 32, :].reshape(4, 8, 128) * mode[d][None]
                            total = term if total is None else total + term
                        target[row, at] = source[row, at] + table[row, at] * total.reshape(32, 128)

            leave[i].start()
        turned = dot(stacked(pack[768:960, :]), right_form(misc[ROW_C : ROW_C + 128, :]))
        ours_pt = left_form(misc[ROW_C + 384 : ROW_C + 512, :])
        product = dot(ours_pt, columns(turned[0:96, :], turned[96:192, :]))
        for s in range(2):
            for e, plane in enumerate(planes_of(product, s)):
                at = (3 * s + e) * 32
                layers_out[at : at + 32, :] = plane

    for copy in leave:
        copy.wait()


def local(state_now, state_prev, pml_flags, interfaces):
    gain, misc, stencil, modes = (jnp.asarray(a) for a in constants())
    smem = pl.BlockSpec(memory_space=pltpu.SMEM)
    whole = pl.BlockSpec(memory_space=pltpu.VMEM)
    hbm = pl.BlockSpec(memory_space=pltpu.HBM)
    free, pack = pl.pallas_call(
        exchange,
        out_shape=(
            jax.ShapeDtypeStruct((S0, CROSS), F32),
            jax.ShapeDtypeStruct((960, 128), F32),
        ),
        in_specs=[smem] + [hbm] * 7,
        out_specs=(pl.BlockSpec(memory_space=pl.ANY),) * 2,
        scratch_shapes=[
            pltpu.VMEM((2, S0, CROSS + 256), F32),
            pltpu.VMEM((S0, CROSS), F32),
            pltpu.VMEM((S0, CROSS), F32),
            pltpu.VMEM(misc.shape, F32),
            pltpu.VMEM(modes.shape, BF16),
            pltpu.VMEM(stencil.shape, BF16),
            pltpu.VMEM((256, CROSS), BF16),
            pltpu.VMEM((S0, CROSS + 512), F32),
            pltpu.VMEM((2, 128, 256), F32),
            pltpu.VMEM((2, 128, 128), F32),
            pltpu.VMEM((768, 128), F32),
            pltpu.VMEM((512, 128), F32),
            pltpu.VMEM((192, 128), F32),
            pltpu.VMEM((3, 128, 384), BF16),
            pltpu.VMEM((5, 384, 128), BF16),
            pltpu.VMEM((8, 128), F32),
            pltpu.VMEM((3, 8, 128), F32),
            pltpu.VMEM((STEPS + 1, 192, 128), F32),
            pltpu.VMEM((STEPS, 3, 96, 128), F32),
            pltpu.VMEM((STEPS, 3, 96, 128), F32),
            pltpu.VMEM((STEPS, 3, 96, 128), F32),
            pltpu.VMEM((960, 128), F32),
            pltpu.SMEM((2, 6), jnp.int32),
            pltpu.SemaphoreType.DMA((10,)),
            pltpu.SemaphoreType.DMA((21,)),
            pltpu.SemaphoreType.DMA((21,)),
            pltpu.SemaphoreType.DMA((2,)),
        ],
        compiler_params=pltpu.CompilerParams(
            collective_id=0, has_side_effects=True, vmem_limit_bytes=32 * 1024 * 1024
        ),
    )(
        pml_flags,
        *(
            pltpu.with_memory_space_constraint(x, pltpu.HBM)
            for x in (interfaces, state_now, state_prev, gain, misc, stencil, modes)
        ),
    )

    new_state, planes = pl.pallas_call(
        close,
        out_shape=(
            jax.ShapeDtypeStruct((1, S0, CROSS), F32),
            jax.ShapeDtypeStruct((192, 128), F32),
        ),
        in_specs=[smem] + [whole] * 4,
        out_specs=(hbm, whole),
        scratch_shapes=[pltpu.VMEM((S0, CROSS), F32), pltpu.SemaphoreType.DMA((PARTS,))],
        compiler_params=pltpu.CompilerParams(vmem_limit_bytes=24 * 1024 * 1024),
    )(pml_flags, pack, misc, free, gain)
    return new_state, planes.reshape(1, 6, CROSS)


def solution(mesh):
    one, two, three = P(("gx", "gy")), P(("gx", "gy"), None), P(("gx", "gy"), None, None)
    return jax.shard_map(
        local,
        mesh=mesh,
        in_specs=(three, three, one, two),
        out_specs=(three, three),
        check_vma=False,
    )
```

```python
import math

import jax
import jax.numpy as jnp
import numpy as np
from jax import lax
from jax.experimental import pallas as pl
from jax.experimental.pallas import tpu as pltpu
from jax.sharding import PartitionSpec as P

S0 = 128
S1 = 64
S2 = 64
CROSS = S1 * S2
STEPS = 3
TILES = CROSS // 128
PLANE = 32
MESH = pl.DeviceIdType.MESH
F32 = jnp.float32
BF16 = jnp.bfloat16

COURANT2 = 0.16
CENTER3 = 3.0 * (-490.0 / 180.0)
TAPS = (1.5, -0.15, 1.0 / 90.0)
TAPS_90 = (135.0, -13.5, 1.0)
PAIRS = {(0, 0): 0, (0, 1): 1, (0, 2): 2, (1, 1): 3, (1, 2): 4, (2, 2): 5}


def basis(n):
    k = np.arange(n)[:, None]
    i = np.arange(n)[None, :]
    weight = np.where(k == 0, math.sqrt(1.0 / n), math.sqrt(2.0 / n))
    return weight * np.cos(math.pi * k * (i + 0.5) / n)


def twice(a):
    n = a.shape[0]
    out = np.zeros((2 * n, 2 * n))
    out[:n, :n] = a
    out[n:, n:] = a
    return out


def constants():
    c0, c1 = basis(S0), basis(S1)
    k = (math.pi * np.arange(S0) / S0) ** 2
    a = (math.pi * np.arange(S1) / S1) ** 2
    wave = (k[:, None, None] + a[None, :, None] + a[None, None, :]).reshape(S0, CROSS)
    safe = np.where(wave > 0, wave, 1.0)
    gain = np.where(wave > 0, 4.0 * np.sin(0.2 * np.sqrt(wave)) ** 2 / safe, COURANT2)
    face = c0[:, :3]
    sign = (-1.0) ** np.arange(S0)
    planes = []
    for s in (np.ones(S0), sign):
        for d, e in PAIRS:
            planes.append(((face[:, d] * face[:, e] * s) @ gain).reshape(PLANE, 128))
    order = np.concatenate([np.arange(0, S1, 2), np.arange(1, S1, 2)])
    c1p = c1[order][:, order]
    misc = np.concatenate(
        [np.repeat(face[:, d : d + 1], 128, axis=1) for d in range(3)]
        + planes
        + [twice(c1), twice(c1.T), twice(c1p), twice(c1p.T)],
        axis=0,
    )

    def band(n):
        out = np.zeros((n, n))
        for distance, tap in enumerate(TAPS_90, 1):
            out += tap * (np.eye(n, k=distance) + np.eye(n, k=-distance))
        return out

    along = band(S0)
    stencil = np.concatenate([np.concatenate([along, along], axis=1), twice(twice(band(S2)))], axis=0)
    six = np.zeros((S0, 8))
    six[:, 0:6] = c0[:, [0, 1, 2, 127, 126, 125]]
    high = six.astype(np.float32).astype(BF16)
    low = (six - high.astype(np.float64)).astype(np.float32).astype(BF16)
    modes = np.concatenate([high, high, low, np.zeros((S0, 8), BF16)], axis=1)
    return gain.astype(np.float32), misc.astype(np.float32), stencil.astype(BF16), modes


ROW_FACE, ROW_P, ROW_C = 0, 384, 768


def rate_of(row):
    return 0.5 * ((row + 0.5) / S0) ** 2


FACE_COEF = [COURANT2 / (1.0 + rate_of(i)) for i in (0, 1, 2, 127, 126, 125)]


def split(x):
    high = x.astype(BF16)
    return high, (x - high.astype(F32)).astype(BF16)


def dot(a, b):
    return jnp.dot(a, b, preferred_element_type=F32)


def couple(p):
    w1, w2, w3 = TAPS
    return [w1 * p[0] + w2 * p[1] + w3 * p[2], w2 * p[0] + w3 * p[1], w3 * p[0]]


def stacked(x):
    hi, lo = split(x)
    return jnp.concatenate([hi, lo, hi], axis=1)


def first_half():
    return lax.broadcasted_iota(jnp.int32, (PLANE, 128), 1) < 64


def columns(*sets):
    first = first_half()
    outer = []
    for w in sets:
        even, odd = [], []
        for e in range(3):
            p = w[e * 32 : (e + 1) * 32, :]
            swapped = pltpu.roll(p, 64, 1)
            even.append(jnp.where(first, p, swapped))
            odd.append(jnp.where(first, swapped, p))
        outer.append(jnp.concatenate(even, axis=1))
        outer.append(jnp.concatenate(odd, axis=1))
    hi, lo = split(jnp.concatenate(outer, axis=0))
    return jnp.concatenate([hi, lo, hi], axis=0)


def planes_of(product, s):
    first = first_half()
    top = product[64 * s : 64 * s + 32, :]
    bottom = product[64 * s + 32 : 64 * s + 64, :]
    return [
        jnp.where(first, top[:, e * 128 : (e + 1) * 128], bottom[:, e * 128 : (e + 1) * 128])
        for e in range(3)
    ]


def left_form(matrix):
    hi, lo = split(matrix)
    return jnp.concatenate([hi, hi, lo], axis=1)


def right_form(matrix):
    hi, lo = split(matrix)
    return jnp.concatenate([hi, hi, lo], axis=0)


def exchange(
    flags, faces_hbm, now_hbm, prev_hbm, gain_hbm, misc_hbm, stencil_hbm, modes_hbm,
    free_out, pack_out,
    state, gain, slow, misc, modes, stencil, halved, rolled, tapped, rows,
    acc, picked, free, left, right, flag_out, flag_in, layers, sums, low_in, force_in, pack,
    faces, load_sem, send_sem, recv_sem, out_sem,
):
    gx, gy = lax.axis_index("gx"), lax.axis_index("gy")
    nx, ny = lax.axis_size("gx"), lax.axis_size("gy")

    head = pltpu.make_async_copy(misc_hbm, misc, load_sem.at[0])
    head.start()
    listed = pltpu.make_async_copy(faces_hbm, faces, load_sem.at[8])
    listed.start()
    chunk = CROSS // 4
    nows = [
        pltpu.make_async_copy(
            now_hbm.at[0, :, pl.ds(i * chunk, chunk)],
            state.at[0, :, pl.ds(128 + i * chunk, chunk)],
            load_sem.at[4 + i],
        )
        for i in range(4)
    ]
    for load in nows:
        load.start()
    rest = [
        pltpu.make_async_copy(gain_hbm, gain, load_sem.at[1]),
        pltpu.make_async_copy(prev_hbm.at[0], state.at[1, :, pl.ds(128, CROSS)], load_sem.at[2]),
        pltpu.make_async_copy(stencil_hbm, stencil, load_sem.at[3]),
        pltpu.make_async_copy(modes_hbm, modes, load_sem.at[9]),
    ]
    for load in rest:
        load.start()
    back_ok, ahead_ok = gx > 0, gx < nx - 1
    side_ok = {-1: gy > 0, 0: gy >= 0, 1: gy < ny - 1}
    barrier = pltpu.get_barrier_semaphore()
    for ok, to_x in ((back_ok, gx - 1), (ahead_ok, gx + 1)):
        for side in (-1, 0, 1):

            @pl.when(jnp.logical_and(ok, side_ok[side]))
            def _():
                pl.semaphore_signal(barrier, inc=1, device_id=(to_x, gy + side), device_id_type=MESH)

    flag_out[...] = jnp.full(flag_out.shape, flags[0], jnp.int32).astype(F32)

    core = lax.rem(gy, 2)
    away = 2 * core - 1
    away_ok = jnp.where(core == 0, gy > 0, gy < ny - 1)
    order = ((away, away_ok), (-away, gy >= 0), (0, gy >= 0))

    def back(source, target, sem, g):
        return pltpu.make_async_remote_copy(
            src_ref=source, dst_ref=target, send_sem=send_sem.at[sem], recv_sem=recv_sem.at[sem],
            device_id=(gx - 1, gy - g), device_id_type=MESH,
        )

    def ahead(source, target, sem, g):
        return pltpu.make_async_remote_copy(
            src_ref=source, dst_ref=target, send_sem=send_sem.at[sem], recv_sem=recv_sem.at[sem],
            device_id=(gx + 1, gy + g), device_id_type=MESH,
        )

    def flag_copy(g):
        return back(flag_out, flag_in.at[g + 1], g + 1, g)

    def low_copy(n, g):
        return back(layers.at[n, pl.ds(0, 96)], low_in.at[n, g + 1], 3 + 3 * n + g + 1, g)

    def force_copy(n, g):
        return ahead(sums.at[n, g + 1], force_in.at[n, g + 1], 12 + 3 * n + g + 1, g)

    def send_back(copy):
        for side, ok in order:

            @pl.when(jnp.logical_and(back_ok, ok))
            def _():
                copy(-side).start()

    def got_back(copy):
        for g in (-1, 0, 1):

            @pl.when(jnp.logical_and(ahead_ok, side_ok[g]))
            def _():
                copy(g).wait_recv()

    def send_ahead(copy):
        for side, ok in order:

            @pl.when(jnp.logical_and(ahead_ok, ok))
            def _():
                copy(side).start()

    def got_ahead(copy):
        for g in (-1, 0, 1):

            @pl.when(jnp.logical_and(back_ok, side_ok[-g]))
            def _():
                copy(g).wait_recv()

    def is_pml(shape):
        return jnp.full(shape, flags[0], jnp.int32) > 0

    listed.wait()
    head.wait()
    big_row = lax.broadcasted_iota(jnp.int32, (128, 128), 0)
    big_col = lax.broadcasted_iota(jnp.int32, (128, 128), 1)
    same = (big_row >> 6) == (big_col >> 6)
    eye = jnp.where(big_row == big_col, 1.0, 0.0).astype(F32)
    own = is_pml((128, 128))
    basis_c, basis_ct, basis_p, basis_pt = (
        misc[ROW_C + i * 128 : ROW_C + (i + 1) * 128, :] for i in range(4)
    )
    ours, ours_t, ours_p, ours_pt = (
        jnp.where(own, eye, m) for m in (basis_c, basis_ct, basis_p, basis_pt)
    )
    q_row, q_col = big_row & 63, big_col & 63
    j_row = 2 * (q_row & 31) + (q_row >> 5)
    j_col = 2 * (q_col & 31) + (q_col >> 5)
    upper = big_row < 64
    step_one = jnp.where(
        upper,
        jnp.full((128, 128), faces[0, 3], jnp.int32),
        jnp.full((128, 128), faces[1, 3], jnp.int32),
    )

    def one_hot(where):
        return jnp.where(where, 1.0, 0.0).astype(BF16)

    def by_exact(a, b):
        hi, lo = split(a)
        return dot(jnp.concatenate([hi, lo], axis=1), jnp.concatenate([b, b], axis=0))

    def exact_by(a, b):
        hi, lo = split(b)
        return dot(jnp.concatenate([a, a], axis=1), jnp.concatenate([hi, lo], axis=0))

    one_pml = by_exact(ours_p, one_hot(jnp.logical_and(same, j_col == j_row - step_one)))
    one_air = dot(stacked(one_pml), right_form(basis_pt))
    two_pml, two_air = [], []
    for r in range(2):
        step_two = jnp.full((128, 128), faces[r, 4], jnp.int32)
        two_pml.append(exact_by(one_hot(jnp.logical_and(same, q_row == q_col - step_two)), ours_t))
        two_air.append(dot(stacked(basis_c), right_form(two_pml[r])))

    left[1] = left_form(one_pml.T)
    right[2] = right_form(two_pml[0].T)
    right[3] = right_form(two_pml[1].T)

    sides = 1 + (gy > 0).astype(jnp.int32) + (gy < ny - 1).astype(jnp.int32)
    ends = (gx > 0).astype(jnp.int32) + (gx < nx - 1).astype(jnp.int32)
    pl.semaphore_wait(barrier, sides * ends)
    send_back(flag_copy)

    line = lax.broadcasted_iota(jnp.int32, (8, 128), 0)

    def note_faces(partial, top, bottom, c):
        full = []
        for d in range(3):
            v = partial[d] + pltpu.roll(partial[d], 4, 0)
            full.append(v + pltpu.roll(v, 2, 0))
        at = pl.ds(pl.multiple_of(c * 8, 8), 8)
        acc[at, :] = jnp.where(line < 2, full[0], jnp.where(line < 4, full[1], full[2]))
        picked[at, :] = jnp.where(line < 4, top, bottom)

    def face_part(partial, chunk_rows, r):
        tiles = chunk_rows.reshape(4, 8, 128)
        out = []
        for d in range(3):
            at = ROW_FACE + d * 128 + 32 * r
            weights = misc[at : at + 32, :].reshape(4, 8, 128)
            term = jnp.sum(weights * tiles, axis=0)
            out.append(term if partial is None else partial[d] + term)
        return out

    def gathered_faces():
        low, high = [], []
        pml = is_pml((PLANE, 128))
        for d in range(3):
            even = acc[pl.ds(2 * d, PLANE, stride=8), :]
            odd = acc[pl.ds(2 * d + 1, PLANE, stride=8), :]
            row_low = picked[pl.ds(d, PLANE, stride=8), :]
            row_high = picked[pl.ds(7 - d, PLANE, stride=8), :]
            low.append(jnp.where(pml, row_low, even + odd))
            high.append(jnp.where(pml, row_high, even - odd))
        return low + high

    for i in range(4):
        nows[i].wait()

        @pl.loop(0, TILES // 8)
        def _(t):
            window = state.at[0, :, pl.ds(pl.multiple_of(128 + i * chunk + t * 256, 128), 256)]
            ats = [slice(h * 128, (h + 1) * 128) for h in range(2)]
            partial = [None, None]
            for r in range(4):
                for h in range(2):
                    partial[h] = face_part(partial[h], window[32 * r : 32 * r + 32, ats[h]], r)
            for h in range(2):
                note_faces(partial[h], window[0:8, ats[h]], window[120:128, ats[h]], 8 * i + 2 * t + h)

    for e, plane in enumerate(gathered_faces()):
        layers[0, e * 32 : (e + 1) * 32, :] = plane
    send_back(lambda g: low_copy(0, g))

    def chosen(r, g):
        return jnp.logical_and(
            jnp.full((96, 128), faces[r, 2], jnp.int32) == g,
            jnp.full((96, 128), faces[r, 5], jnp.int32) > 0,
        )

    def make_sums(n):
        z = couple([layers[n, (3 + d) * 32 : (4 + d) * 32, :] for d in range(3)])
        z3 = stacked(jnp.concatenate(z, axis=0))
        product = dot(left[1], columns(dot(z3, right[2]), dot(z3, right[3])))
        moved = [jnp.concatenate(planes_of(product, r), axis=0) for r in range(2)]
        for g in (-1, 0, 1):
            total = jnp.where(chosen(0, g), moved[0], 0.0) + jnp.where(chosen(1, g), moved[1], 0.0)
            sums[n, g + 1] = total

    def high_force(n):
        parts = []
        for r in range(2):
            pick = jnp.zeros((96, 128), F32)
            for g in (-1, 0, 1):
                pick = jnp.where(chosen(r, g), low_in[n, g + 1], pick)
            parts.append(dot(stacked(pick), right[r]))
        product = dot(left[0], columns(parts[0], parts[1]))
        a, b = planes_of(product, 0), planes_of(product, 1)
        return couple([x + y for x, y in zip(a, b)])

    def low_force(n):
        total = jnp.zeros((96, 128), F32)
        for g in (-1, 0, 1):
            there = jnp.logical_and(back_ok, side_ok[-g]).astype(jnp.int32)
            total += jnp.where(jnp.full((96, 128), there, jnp.int32) > 0, force_in[n, g + 1], 0.0)
        return total

    def response(force):
        pml = is_pml((PLANE, 128))
        low, high = [], []
        for d in range(3):
            near, far = 0.0, 0.0
            for e in range(3):
                i = PAIRS[(min(d, e), max(d, e))]
                p = misc[ROW_P + i * 32 : ROW_P + (i + 1) * 32, :]
                q = misc[ROW_P + 192 + i * 32 : ROW_P + 192 + (i + 1) * 32, :]
                near = near + (p * force[e] + q * force[3 + e])
                far = far + (q * force[e] + p * force[3 + e])
            low.append(jnp.where(pml, FACE_COEF[d] * force[d], near))
            high.append(jnp.where(pml, FACE_COEF[3 + d] * force[3 + d], far))
        return low + high

    make_sums(0)
    send_ahead(lambda g: force_copy(0, g))
    k = big_row.astype(F32)
    rate = 0.5 * ((k + 0.5) * (1.0 / S0)) ** 2
    inverse = 1.0 / (1.0 + rate)
    rows[0] = jnp.where(own, (1.0 - rate) * inverse, 1.0)
    rows[1] = jnp.where(own, (COURANT2 / 90.0) * inverse, 0.0)
    center = (2.0 + COURANT2 * CENTER3) * inverse
    mode_k = (k * (math.pi / S0)) * (k * (math.pi / S0))
    edge = jnp.zeros((S0, 128), F32)
    for b in range(2):
        state[b, :, 0:128] = edge
        state[b, :, 128 + CROSS : 256 + CROSS] = edge
    for c in (0, 1, TILES + 2, TILES + 3):
        rolled[:, c * 128 : (c + 1) * 128] = edge
    pack[192:768, :] = jnp.zeros((576, 128), F32)
    rest[0].wait()

    def tile(c):
        return pl.ds(pl.multiple_of(c * 128, 128), 128)

    @pl.loop(0, TILES)
    def _(c):
        col = c * 128 + lax.broadcasted_iota(jnp.int32, (1, 128), 1)
        mode_a = (col >> 6).astype(F32) * (math.pi / S1)
        mode_b = (col & 63).astype(F32) * (math.pi / S2)
        wave = mode_k + (mode_a * mode_a + mode_b * mode_b)
        slow[:, tile(c)] = jnp.where(own, center, 2.0 - gain[:, tile(c)] * wave)

    rest[1].wait()
    rest[2].wait()
    rest[3].wait()

    def keep_force(force):
        pml = is_pml((PLANE, 128))
        for d in range(3):
            pack[d * 32 : (d + 1) * 32, :] = jnp.where(pml, 0.0, force[d])
            pack[96 + d * 32 : 96 + (d + 1) * 32, :] = jnp.where(pml, 0.0, force[3 + d])
            pack[256 + d * 32 : 256 + (d + 1) * 32, :] = jnp.where(pml, FACE_COEF[d] * force[d], 0.0)
            at = 512 + (7 - d) * 32
            pack[at : at + 32, :] = jnp.where(pml, FACE_COEF[3 + d] * force[3 + d], 0.0)

    def finish(box, table, cut, turn, at, c0, n):
        if n > 0:
            along_box = spread_modes(modes, pack, c0)
            top = both(pack, 256, c0)
            bottom = both(pack, 512, c0)
        for r in range(4):
            row = slice(32 * r, 32 * r + 32)
            for h in range(2):
                here = slice(at + h * 128, at + (h + 1) * 128)
                box_here = slice(at + 128 + h * 128, at + 256 + h * 128)
                turn_here = slice(at + 256 + h * 128, at + 384 + h * 128)
                side = slice(h * 128, (h + 1) * 128)
                block = box[row, box_here]
                if n > 0:
                    block = block + table[row, here] * along_box[row, side]
                    if r == 0:
                        block = jnp.concatenate([block[0:8] + top[:, side], block[8:32]], axis=0)
                    if r == 3:
                        block = jnp.concatenate([block[0:24], block[24:32] + bottom[:, side]], axis=0)
                    box[row, box_here] = block
                hi, lo = split(block)
                cut[row, here] = hi
                cut[slice(128 + 32 * r, 160 + 32 * r), here] = lo
                turn[row, turn_here] = pltpu.roll(block, 64, 1)

    w1, w2 = TAPS_90[0], TAPS_90[1]
    small_first = lax.broadcasted_iota(jnp.int32, (32, 128), 1) < 64

    def keep_taps(cut, at, slot):
        pair = cut[:, at : at + 256]
        operand = jnp.concatenate([stencil[0:128, :], pair[0:128, :], pair[128:256, :]], axis=1)
        fixed = stencil[128:384, :]
        tapped[slot] = dot(operand, jnp.concatenate([pair, fixed, fixed], axis=0))

    def advance(b, p, n):
        def step(base, c0, at, slot, ahead_by, width):
            box = state.at[b, :, pl.ds(base, 256 + width)]
            old = state.at[p, :, pl.ds(base, 256 + width)]
            turn = rolled.at[:, pl.ds(base, 512 + width)]
            cut = halved.at[:, pl.ds(base, width)]
            table = gain.at[:, pl.ds(base, width)]
            own_slow = slow.at[:, pl.ds(base, width)]
            if ahead_by > 0:
                keep_taps(cut, at + 256, 1 - slot)
            if ahead_by > 1:
                finish(box, table, cut, turn, at + 512, c0 + 4, n)
            partial = [None, None]
            ends_ = [[None, None], [None, None]]
            for r in range(4):
                row = slice(32 * r, 32 * r + 32)
                ring = [turn[row, at + i * 128 : at + (i + 1) * 128] for i in range(6)]
                line = [box[row, at + i * 128 : at + (i + 1) * 128] for i in range(4)]
                quads = [w1 * (ring[i + 2] + ring[i + 1]) + (ring[i + 3] + ring[i]) for i in range(3)]
                for h in range(2):
                    here = slice(at + h * 128, at + (h + 1) * 128)
                    box_here = slice(at + 128 + h * 128, at + 256 + h * 128)
                    total = tapped[slot, row, h * 128 : (h + 1) * 128] + w2 * (line[h] + line[h + 2])
                    total += jnp.where(small_first, quads[h], quads[h + 1])
                    following = own_slow[row, here] * line[h + 1]
                    following -= rows[0, row, :] * old[row, box_here]
                    following += rows[1, row, :] * total
                    old[row, box_here] = following
                    partial[h] = face_part(partial[h], following, r)
                    if r == 0:
                        ends_[h][0] = following[0:8]
                    if r == 3:
                        ends_[h][1] = following[24:32]
            for h in range(2):
                note_faces(partial[h], ends_[h][0], ends_[h][1], c0 + h)

        for t in range(2):
            base = t * 256
            finish(
                state.at[b, :, pl.ds(base, 512)], gain.at[:, pl.ds(base, 256)], halved.at[:, pl.ds(base, 256)],
                rolled.at[:, pl.ds(base, 768)], 0, 2 * t, n,
            )
        keep_taps(halved, 0, 0)

        @pl.loop(0, TILES // 4 - 1)
        def _(i):
            base = pl.multiple_of(i * 512, 512)
            for s in range(2):
                step(base, 4 * i + 2 * s, 256 * s, s, 2, 1024)

        base = CROSS - 512
        step(base, TILES - 4, 0, 0, 1, 512)
        step(base, TILES - 2, 256, 1, 0, 512)

        for e, plane in enumerate(gathered_faces()):
            free[e * 32 : (e + 1) * 32, :] = plane

    def theirs(r):
        g = jnp.full((8, 128), faces[r, 2], jnp.int32)
        value = jnp.where(g == -1, flag_in[0], jnp.where(g == 0, flag_in[1], flag_in[2]))
        return jnp.broadcast_to(value[0:1, :], (128, 128))

    def finish_matrices():
        got_back(flag_copy)
        their = [theirs(r) for r in range(2)]
        their_col = jnp.where(big_col < 64, their[0], their[1]) > 0.5
        cross_one = jnp.where(their_col, one_pml, one_air)
        left[0] = left_form(cross_one)
        left[1] = left_form(cross_one.T)
        for r in range(2):
            cross_two = jnp.where(their[r] > 0.5, two_pml[r], two_air[r])
            right[r] = right_form(cross_two)
            right[2 + r] = right_form(cross_two.T)
        left[2] = left_form(ours_p)
        right[4] = right_form(ours_t)

    unforced = pltpu.make_async_copy(
        state.at[STEPS % 2, :, pl.ds(128, CROSS)], free_out, out_sem.at[0]
    )
    for n in range(STEPS):
        b, p = n % 2, 1 - n % 2
        if n > 0:
            send_back(lambda g: low_copy(n, g))
            make_sums(n)
            send_ahead(lambda g: force_copy(n, g))
            keep_force(force)
        advance(b, p, n)
        if n == 0:
            finish_matrices()
        if n == STEPS - 1:
            unforced.start()
        got_back(lambda g: low_copy(n, g))
        high = high_force(n)
        got_ahead(lambda g: force_copy(n, g))
        low = low_force(n)
        if n == 0:
            turned = dot(stacked(low), right[4])
            low = planes_of(dot(left[2], columns(turned, jnp.zeros((96, 128), F32))), 0)
        else:
            low = [low[e * 32 : (e + 1) * 32, :] for e in range(3)]
        force = low + high
        for e, plane in enumerate(response(force)):
            at = slice(e * 32, (e + 1) * 32)
            layers[n + 1, at, :] = free[at, :] + plane

    keep_force(force)
    pack[768:960, :] = layers[STEPS]
    packed = pltpu.make_async_copy(pack, pack_out, out_sem.at[1])
    packed.start()

    for side, ok in order:

        @pl.when(jnp.logical_and(back_ok, ok))
        def _():
            flag_copy(-side).wait_send()
            for n in range(STEPS):
                low_copy(n, -side).wait_send()

        @pl.when(jnp.logical_and(ahead_ok, ok))
        def _():
            for n in range(STEPS):
                force_copy(n, side).wait_send()

    unforced.wait()
    packed.wait()


def both(pack, row, c):
    return jnp.concatenate([pack[pl.ds(row + c + h, 8, stride=PLANE), :] for h in range(2)], axis=1)


def spread_modes(modes, pack, c):
    hi, lo = split(both(pack, 0, c))
    hi = hi.astype(F32)
    terms = jnp.concatenate([hi, lo.astype(F32), hi, jnp.zeros((8, 256), F32)], axis=0)
    return dot(modes[...], terms.astype(BF16))


PARTS = 8
WIDE = CROSS // PARTS


def close(flags, pack, misc, free, gain, out, layers_out, done, sems):
    pml = flags[0] > 0
    leave = [
        pltpu.make_async_copy(
            done.at[:, pl.ds(i * WIDE, WIDE)], out.at[0, :, pl.ds(i * WIDE, WIDE)], sems.at[i]
        )
        for i in range(PARTS)
    ]

    @pl.when(pml)
    def _():
        for i in range(PARTS):
            at = slice(i * WIDE, (i + 1) * WIDE)
            done[:, at] = free[:, at]
            for h in range(WIDE // 128):
                c = i * (WIDE // 128) + h
                at = slice(c * 128, (c + 1) * 128)
                done[0:8, at] = free[0:8, at] + pack[pl.ds(256 + c, 8, stride=PLANE), :]
                done[120:128, at] = free[120:128, at] + pack[pl.ds(512 + c, 8, stride=PLANE), :]
            leave[i].start()
        layers_out[...] = pack[768:960, :]

    @pl.when(jnp.logical_not(pml))
    def _():
        even = (lax.broadcasted_iota(jnp.int32, (8, 128), 0) & 1) == 0
        for i in range(PARTS):

            @pl.loop(0, WIDE // 256)
            def _(t):
                window = pl.ds(pl.multiple_of(i * WIDE + t * 256, 256), 256)
                source, table, target = free.at[:, window], gain.at[:, window], done.at[:, window]
                modes = []
                for h in range(2):
                    c = i * (WIDE // 128) + 2 * t + h
                    mode = []
                    for d in range(3):
                        low = jnp.broadcast_to(pack[pl.ds(d * 32 + c, 1), :], (8, 128))
                        high = jnp.broadcast_to(pack[pl.ds(96 + d * 32 + c, 1), :], (8, 128))
                        mode.append(low + jnp.where(even, high, -high))
                    modes.append(mode)
                for r in range(8):
                    row = slice(16 * r, 16 * r + 16)
                    weights = [
                        misc[ROW_FACE + d * 128 + 16 * r : ROW_FACE + d * 128 + 16 * r + 16, :].reshape(2, 8, 128)
                        for d in range(3)
                    ]
                    for h in range(2):
                        at = slice(h * 128, (h + 1) * 128)
                        total = sum(weights[d] * modes[h][d][None] for d in range(3))
                        target[row, at] = source[row, at] + table[row, at] * total.reshape(16, 128)

            leave[i].start()
        turned = dot(stacked(pack[768:960, :]), right_form(misc[ROW_C : ROW_C + 128, :]))
        ours_pt = left_form(misc[ROW_C + 384 : ROW_C + 512, :])
        product = dot(ours_pt, columns(turned[0:96, :], turned[96:192, :]))
        for s in range(2):
            for e, plane in enumerate(planes_of(product, s)):
                at = (3 * s + e) * 32
                layers_out[at : at + 32, :] = plane

    for copy in leave:
        copy.wait()


def local(state_now, state_prev, pml_flags, interfaces):
    gain, misc, stencil, modes = (jnp.asarray(a) for a in constants())
    smem = pl.BlockSpec(memory_space=pltpu.SMEM)
    whole = pl.BlockSpec(memory_space=pltpu.VMEM)
    hbm = pl.BlockSpec(memory_space=pltpu.HBM)
    free, pack = pl.pallas_call(
        exchange,
        out_shape=(
            jax.ShapeDtypeStruct((S0, CROSS), F32),
            jax.ShapeDtypeStruct((960, 128), F32),
        ),
        in_specs=[smem] + [hbm] * 7,
        out_specs=(pl.BlockSpec(memory_space=pl.ANY),) * 2,
        scratch_shapes=[
            pltpu.VMEM((2, S0, CROSS + 256), F32),
            pltpu.VMEM((S0, CROSS), F32),
            pltpu.VMEM((S0, CROSS), F32),
            pltpu.VMEM(misc.shape, F32),
            pltpu.VMEM(modes.shape, BF16),
            pltpu.VMEM(stencil.shape, BF16),
            pltpu.VMEM((256, CROSS), BF16),
            pltpu.VMEM((S0, CROSS + 512), F32),
            pltpu.VMEM((2, 128, 256), F32),
            pltpu.VMEM((2, 128, 128), F32),
            pltpu.VMEM((256, 128), F32),
            pltpu.VMEM((256, 128), F32),
            pltpu.VMEM((192, 128), F32),
            pltpu.VMEM((3, 128, 384), BF16),
            pltpu.VMEM((5, 384, 128), BF16),
            pltpu.VMEM((8, 128), F32),
            pltpu.VMEM((3, 8, 128), F32),
            pltpu.VMEM((STEPS + 1, 192, 128), F32),
            pltpu.VMEM((STEPS, 3, 96, 128), F32),
            pltpu.VMEM((STEPS, 3, 96, 128), F32),
            pltpu.VMEM((STEPS, 3, 96, 128), F32),
            pltpu.VMEM((960, 128), F32),
            pltpu.SMEM((2, 6), jnp.int32),
            pltpu.SemaphoreType.DMA((10,)),
            pltpu.SemaphoreType.DMA((21,)),
            pltpu.SemaphoreType.DMA((21,)),
            pltpu.SemaphoreType.DMA((2,)),
        ],
        compiler_params=pltpu.CompilerParams(
            collective_id=0, has_side_effects=True, vmem_limit_bytes=32 * 1024 * 1024
        ),
    )(
        pml_flags,
        *(
            pltpu.with_memory_space_constraint(x, pltpu.HBM)
            for x in (interfaces, state_now, state_prev, gain, misc, stencil, modes)
        ),
    )

    new_state, planes = pl.pallas_call(
        close,
        out_shape=(
            jax.ShapeDtypeStruct((1, S0, CROSS), F32),
            jax.ShapeDtypeStruct((192, 128), F32),
        ),
        in_specs=[smem] + [whole] * 4,
        out_specs=(hbm, whole),
        scratch_shapes=[pltpu.VMEM((S0, CROSS), F32), pltpu.SemaphoreType.DMA((PARTS,))],
        compiler_params=pltpu.CompilerParams(vmem_limit_bytes=24 * 1024 * 1024),
    )(pml_flags, pack, misc, free, gain)
    return new_state, planes.reshape(1, 6, CROSS)


def solution(mesh):
    one, two, three = P(("gx", "gy")), P(("gx", "gy"), None), P(("gx", "gy"), None, None)
    return jax.shard_map(
        local,
        mesh=mesh,
        in_specs=(three, three, one, two),
        out_specs=(three, three),
        check_vma=False,
    )
```

```python
import math

import jax
import jax.numpy as jnp
import numpy as np
from jax import lax
from jax.experimental import pallas as pl
from jax.experimental.pallas import tpu as pltpu
from jax.sharding import PartitionSpec as P

S0 = 128
S1 = 64
S2 = 64
CROSS = S1 * S2
STEPS = 3
FORCES_AT = 1
LAYERS_AT = (4, 5)
TILES = CROSS // 128
PLANE = 32
MESH = pl.DeviceIdType.MESH
F32 = jnp.float32
BF16 = jnp.bfloat16

COURANT2 = 0.16
CENTER3 = 3.0 * (-490.0 / 180.0)
TAPS = (1.5, -0.15, 1.0 / 90.0)
TAPS_90 = (135.0, -13.5, 1.0)
PAIRS = {(0, 0): 0, (0, 1): 1, (0, 2): 2, (1, 1): 3, (1, 2): 4, (2, 2): 5}


def basis(n):
    k = np.arange(n)[:, None]
    i = np.arange(n)[None, :]
    weight = np.where(k == 0, math.sqrt(1.0 / n), math.sqrt(2.0 / n))
    return weight * np.cos(math.pi * k * (i + 0.5) / n)


def twice(a):
    n = a.shape[0]
    out = np.zeros((2 * n, 2 * n))
    out[:n, :n] = a
    out[n:, n:] = a
    return out


def constants():
    c0, c1 = basis(S0), basis(S1)
    k = (math.pi * np.arange(S0) / S0) ** 2
    a = (math.pi * np.arange(S1) / S1) ** 2
    wave = (k[:, None, None] + a[None, :, None] + a[None, None, :]).reshape(S0, CROSS)
    safe = np.where(wave > 0, wave, 1.0)
    gain = np.where(wave > 0, 4.0 * np.sin(0.2 * np.sqrt(wave)) ** 2 / safe, COURANT2)
    face = c0[:, :3]
    sign = (-1.0) ** np.arange(S0)
    planes = []
    for s in (np.ones(S0), sign):
        for d, e in PAIRS:
            planes.append(((face[:, d] * face[:, e] * s) @ gain).reshape(PLANE, 128))
    order = np.concatenate([np.arange(0, S1, 2), np.arange(1, S1, 2)])
    c1p = c1[order][:, order]
    misc = np.concatenate(
        [np.repeat(face[:, d : d + 1], 128, axis=1) for d in range(3)]
        + planes
        + [twice(c1), twice(c1.T), twice(c1p), twice(c1p.T)],
        axis=0,
    )

    def band(n):
        out = np.zeros((n, n))
        for distance, tap in enumerate(TAPS_90, 1):
            out += tap * (np.eye(n, k=distance) + np.eye(n, k=-distance))
        return out

    along = band(S0)
    stencil = np.concatenate([np.concatenate([along, along], axis=1), twice(twice(band(S2)))], axis=0)
    six = np.zeros((S0, 8))
    six[:, 0:6] = c0[:, [0, 1, 2, 127, 126, 125]]
    high = six.astype(np.float32).astype(BF16)
    low = (six - high.astype(np.float64)).astype(np.float32).astype(BF16)
    modes = np.concatenate([high, high, low, np.zeros((S0, 8), BF16)], axis=1)
    return gain.astype(np.float32), misc.astype(np.float32), stencil.astype(BF16), modes


ROW_FACE, ROW_P, ROW_C = 0, 384, 768


def rate_of(row):
    return 0.5 * ((row + 0.5) / S0) ** 2


FACE_COEF = [COURANT2 / (1.0 + rate_of(i)) for i in (0, 1, 2, 127, 126, 125)]


def split(x):
    high = x.astype(BF16)
    return high, (x - high.astype(F32)).astype(BF16)


def dot(a, b):
    return jnp.dot(a, b, preferred_element_type=F32)


def couple(p):
    w1, w2, w3 = TAPS
    return [w1 * p[0] + w2 * p[1] + w3 * p[2], w2 * p[0] + w3 * p[1], w3 * p[0]]


def stacked(x):
    hi, lo = split(x)
    return jnp.concatenate([hi, lo, hi], axis=1)


def first_half():
    return lax.broadcasted_iota(jnp.int32, (PLANE, 128), 1) < 64


def columns(*sets):
    first = first_half()
    outer = []
    for w in sets:
        even, odd = [], []
        for e in range(3):
            p = w[e * 32 : (e + 1) * 32, :]
            swapped = pltpu.roll(p, 64, 1)
            even.append(jnp.where(first, p, swapped))
            odd.append(jnp.where(first, swapped, p))
        outer.append(jnp.concatenate(even, axis=1))
        outer.append(jnp.concatenate(odd, axis=1))
    hi, lo = split(jnp.concatenate(outer, axis=0))
    return jnp.concatenate([hi, lo, hi], axis=0)


def planes_of(product, s):
    first = first_half()
    top = product[64 * s : 64 * s + 32, :]
    bottom = product[64 * s + 32 : 64 * s + 64, :]
    return [
        jnp.where(first, top[:, e * 128 : (e + 1) * 128], bottom[:, e * 128 : (e + 1) * 128])
        for e in range(3)
    ]


def left_form(matrix):
    hi, lo = split(matrix)
    return jnp.concatenate([hi, hi, lo], axis=1)


def right_form(matrix):
    hi, lo = split(matrix)
    return jnp.concatenate([hi, hi, lo], axis=0)


def exchange(
    flags, faces_hbm, now_hbm, prev_hbm, gain_hbm, misc_hbm, stencil_hbm, modes_hbm,
    free_out, pack_out,
    state, gain, slow, misc, modes, stencil, halved, rolled, tapped, rows,
    acc, picked, free, left, right, flag_out, flag_in, layers, sums, low_in, force_in, pair_in, pack,
    faces, load_sem, send_sem, recv_sem, out_sem,
):
    gx, gy = lax.axis_index("gx"), lax.axis_index("gy")
    nx, ny = lax.axis_size("gx"), lax.axis_size("gy")

    head = pltpu.make_async_copy(misc_hbm, misc, load_sem.at[0])
    head.start()
    listed = pltpu.make_async_copy(faces_hbm, faces, load_sem.at[8])
    listed.start()
    chunk = CROSS // 4
    nows = [
        pltpu.make_async_copy(
            now_hbm.at[0, :, pl.ds(i * chunk, chunk)],
            state.at[0, :, pl.ds(128 + i * chunk, chunk)],
            load_sem.at[4 + i],
        )
        for i in range(4)
    ]
    for load in nows:
        load.start()
    rest = [
        pltpu.make_async_copy(gain_hbm, gain, load_sem.at[1]),
        pltpu.make_async_copy(prev_hbm.at[0], state.at[1, :, pl.ds(128, CROSS)], load_sem.at[2]),
        pltpu.make_async_copy(stencil_hbm, stencil, load_sem.at[3]),
        pltpu.make_async_copy(modes_hbm, modes, load_sem.at[9]),
    ]
    for load in rest:
        load.start()
    core = lax.rem(gy, 2)
    away = 2 * core - 1
    other = -away
    away_ok = jnp.where(core == 0, gy > 0, gy < ny - 1)
    order = ((away, away_ok), (other, gy >= 0), (0, gy >= 0))

    back_ok, ahead_ok = gx > 0, gx < nx - 1
    side_ok = {-1: gy > 0, 0: gy >= 0, 1: gy < ny - 1}
    barrier = pltpu.get_barrier_semaphore()
    for ok, to_x in ((back_ok, gx - 1), (ahead_ok, gx + 1)):
        for side in (-1, 0, 1):

            @pl.when(jnp.logical_and(ok, side_ok[side]))
            def _():
                pl.semaphore_signal(barrier, inc=1, device_id=(to_x, gy + side), device_id_type=MESH)

    pl.semaphore_signal(barrier, inc=1, device_id=(gx, gy + other), device_id_type=MESH)
    flag_out[...] = jnp.full(flag_out.shape, flags[0], jnp.int32).astype(F32)

    def send(source, target, sem, to_x, to_y):
        return pltpu.make_async_remote_copy(
            src_ref=source, dst_ref=target, send_sem=send_sem.at[sem], recv_sem=recv_sem.at[sem],
            device_id=(to_x, to_y), device_id_type=MESH,
        )

    def flag_copy(g):
        return send(flag_out, flag_in.at[g + 1], g + 1, gx - 1, gy - g)

    half = (pl.ds(0, 48), pl.ds(48, 48))

    def low_straight(n, h):
        return send(layers.at[n, half[h]], low_in.at[n, 1, half[h]], 3 + 8 * n + h, gx - 1, gy)

    def low_away(n):
        return send(layers.at[n, pl.ds(0, 96)], low_in.at[n, 1 - away], 5 + 8 * n, gx - 1, gy + away)

    def low_other(n):
        return send(layers.at[n, half[0]], low_in.at[n, 1 - other, half[0]], 6 + 8 * n, gx - 1, gy + other)

    def low_relay(n):
        return send(low_in.at[n, 1, half[1]], low_in.at[n, 1 - other, half[1]], 7 + 8 * n, gx, gy + other)

    def force_away(n):
        return send(sums.at[n, away + 1], force_in.at[n, away + 1], 8 + 8 * n, gx + 1, gy + away)

    def force_pair(n):
        return send(sums.at[n, other + 1], pair_in.at[n], 9 + 8 * n, gx, gy + other)

    def force_straight(n):
        return send(sums.at[n, 3], force_in.at[n, 1], 10 + 8 * n, gx + 1, gy)

    def send_back(n):
        @pl.when(back_ok)
        def _():
            low_straight(n, 1).start()

            @pl.when(away_ok)
            def _():
                low_away(n).start()

            low_straight(n, 0).start()
            low_other(n).start()

    def send_ahead(n):
        @pl.when(ahead_ok)
        def _():
            force_pair(n).start()

            @pl.when(away_ok)
            def _():
                force_away(n).start()

    def pass_forces(n):
        force_pair(n).wait_recv()
        sums[n, 3] = sums[n, 1] + pair_in[n]
        force_straight(n).start()

    def pass_layers(n):
        low_straight(n, 1).wait_recv()
        low_relay(n).start()

    def got_back(n):
        @pl.when(ahead_ok)
        def _():
            low_straight(n, 0).wait_recv()
            low_other(n).wait_recv()
            low_relay(n).wait_recv()

            @pl.when(away_ok)
            def _():
                low_away(n).wait_recv()

    def got_ahead(n):
        @pl.when(back_ok)
        def _():
            force_straight(n).wait_recv()

            @pl.when(away_ok)
            def _():
                force_away(n).wait_recv()

    def is_pml(shape):
        return jnp.full(shape, flags[0], jnp.int32) > 0

    listed.wait()
    head.wait()
    big_row = lax.broadcasted_iota(jnp.int32, (128, 128), 0)
    big_col = lax.broadcasted_iota(jnp.int32, (128, 128), 1)
    same = (big_row >> 6) == (big_col >> 6)
    eye = jnp.where(big_row == big_col, 1.0, 0.0).astype(F32)
    own = is_pml((128, 128))
    basis_c, basis_ct, basis_p, basis_pt = (
        misc[ROW_C + i * 128 : ROW_C + (i + 1) * 128, :] for i in range(4)
    )
    ours, ours_t, ours_p, ours_pt = (
        jnp.where(own, eye, m) for m in (basis_c, basis_ct, basis_p, basis_pt)
    )
    q_row, q_col = big_row & 63, big_col & 63
    j_row = 2 * (q_row & 31) + (q_row >> 5)
    j_col = 2 * (q_col & 31) + (q_col >> 5)
    upper = big_row < 64
    step_one = jnp.where(
        upper,
        jnp.full((128, 128), faces[0, 3], jnp.int32),
        jnp.full((128, 128), faces[1, 3], jnp.int32),
    )

    def one_hot(where):
        return jnp.where(where, 1.0, 0.0).astype(BF16)

    def by_exact(a, b):
        hi, lo = split(a)
        return dot(jnp.concatenate([hi, lo], axis=1), jnp.concatenate([b, b], axis=0))

    def exact_by(a, b):
        hi, lo = split(b)
        return dot(jnp.concatenate([a, a], axis=1), jnp.concatenate([hi, lo], axis=0))

    one_pml = by_exact(ours_p, one_hot(jnp.logical_and(same, j_col == j_row - step_one)))
    one_air = dot(stacked(one_pml), right_form(basis_pt))
    two_pml, two_air = [], []
    for r in range(2):
        step_two = jnp.full((128, 128), faces[r, 4], jnp.int32)
        two_pml.append(exact_by(one_hot(jnp.logical_and(same, q_row == q_col - step_two)), ours_t))
        two_air.append(dot(stacked(basis_c), right_form(two_pml[r])))

    left[1] = left_form(one_pml.T)
    right[2] = right_form(two_pml[0].T)
    right[3] = right_form(two_pml[1].T)

    sides = 1 + (gy > 0).astype(jnp.int32) + (gy < ny - 1).astype(jnp.int32)
    ends = (gx > 0).astype(jnp.int32) + (gx < nx - 1).astype(jnp.int32)
    pl.semaphore_wait(barrier, sides * ends + 1)
    for side, ok in order:

        @pl.when(jnp.logical_and(back_ok, ok))
        def _():
            flag_copy(-side).start()


    line = lax.broadcasted_iota(jnp.int32, (8, 128), 0)

    def note_faces(partial, top, bottom, c):
        full = []
        for d in range(3):
            v = partial[d] + pltpu.roll(partial[d], 4, 0)
            full.append(v + pltpu.roll(v, 2, 0))
        at = pl.ds(pl.multiple_of(c * 8, 8), 8)
        acc[at, :] = jnp.where(line < 2, full[0], jnp.where(line < 4, full[1], full[2]))
        picked[at, :] = jnp.where(line < 4, top, bottom)

    def face_part(partial, chunk_rows, r):
        tiles = chunk_rows.reshape(4, 8, 128)
        out = []
        for d in range(3):
            at = ROW_FACE + d * 128 + 32 * r
            weights = misc[at : at + 32, :].reshape(4, 8, 128)
            term = jnp.sum(weights * tiles, axis=0)
            out.append(term if partial is None else partial[d] + term)
        return out

    def gathered_faces():
        low, high = [], []
        pml = is_pml((PLANE, 128))
        for d in range(3):
            even = acc[pl.ds(2 * d, PLANE, stride=8), :]
            odd = acc[pl.ds(2 * d + 1, PLANE, stride=8), :]
            row_low = picked[pl.ds(d, PLANE, stride=8), :]
            row_high = picked[pl.ds(7 - d, PLANE, stride=8), :]
            low.append(jnp.where(pml, row_low, even + odd))
            high.append(jnp.where(pml, row_high, even - odd))
        return low + high

    for i in range(4):
        nows[i].wait()

        @pl.loop(0, TILES // 8)
        def _(t):
            window = state.at[0, :, pl.ds(pl.multiple_of(128 + i * chunk + t * 256, 128), 256)]
            ats = [slice(h * 128, (h + 1) * 128) for h in range(2)]
            partial = [None, None]
            for r in range(4):
                for h in range(2):
                    partial[h] = face_part(partial[h], window[32 * r : 32 * r + 32, ats[h]], r)
            for h in range(2):
                note_faces(partial[h], window[0:8, ats[h]], window[120:128, ats[h]], 8 * i + 2 * t + h)

    for e, plane in enumerate(gathered_faces()):
        layers[0, e * 32 : (e + 1) * 32, :] = plane
    send_back(0)

    def chosen(r, g):
        return jnp.logical_and(
            jnp.full((96, 128), faces[r, 2], jnp.int32) == g,
            jnp.full((96, 128), faces[r, 5], jnp.int32) > 0,
        )

    def make_sums(n):
        z = couple([layers[n, (3 + d) * 32 : (4 + d) * 32, :] for d in range(3)])
        z3 = stacked(jnp.concatenate(z, axis=0))
        product = dot(left[1], columns(dot(z3, right[2]), dot(z3, right[3])))
        moved = [jnp.concatenate(planes_of(product, r), axis=0) for r in range(2)]
        for g in (-1, 0, 1):
            total = jnp.where(chosen(0, g), moved[0], 0.0) + jnp.where(chosen(1, g), moved[1], 0.0)
            sums[n, g + 1] = total

    def high_force(n):
        parts = []
        for r in range(2):
            pick = jnp.zeros((96, 128), F32)
            for g in (-1, 0, 1):
                pick = jnp.where(chosen(r, g), low_in[n, g + 1], pick)
            parts.append(dot(stacked(pick), right[r]))
        product = dot(left[0], columns(parts[0], parts[1]))
        a, b = planes_of(product, 0), planes_of(product, 1)
        return couple([x + y for x, y in zip(a, b)])

    def low_force(n):
        straight_there = jnp.full((96, 128), back_ok.astype(jnp.int32), jnp.int32) > 0
        away_there = jnp.full((96, 128), jnp.logical_and(back_ok, away_ok).astype(jnp.int32), jnp.int32) > 0
        total = jnp.where(straight_there, force_in[n, 1], 0.0)
        total += jnp.where(away_there, force_in[n, 1 - away], 0.0)
        return total

    def response(force):
        pml = is_pml((PLANE, 128))
        low, high = [], []
        for d in range(3):
            near, far = 0.0, 0.0
            for e in range(3):
                i = PAIRS[(min(d, e), max(d, e))]
                p = misc[ROW_P + i * 32 : ROW_P + (i + 1) * 32, :]
                q = misc[ROW_P + 192 + i * 32 : ROW_P + 192 + (i + 1) * 32, :]
                near = near + (p * force[e] + q * force[3 + e])
                far = far + (q * force[e] + p * force[3 + e])
            low.append(jnp.where(pml, FACE_COEF[d] * force[d], near))
            high.append(jnp.where(pml, FACE_COEF[3 + d] * force[3 + d], far))
        return low + high

    make_sums(0)
    send_ahead(0)
    k = big_row.astype(F32)
    rate = 0.5 * ((k + 0.5) * (1.0 / S0)) ** 2
    inverse = 1.0 / (1.0 + rate)
    rows[0] = jnp.where(own, (1.0 - rate) * inverse, 1.0)
    rows[1] = jnp.where(own, (COURANT2 / 90.0) * inverse, 0.0)
    center = (2.0 + COURANT2 * CENTER3) * inverse
    mode_k = (k * (math.pi / S0)) * (k * (math.pi / S0))
    edge = jnp.zeros((S0, 128), F32)
    for b in range(2):
        state[b, :, 0:128] = edge
        state[b, :, 128 + CROSS : 256 + CROSS] = edge
    for c in (0, 1, TILES + 2, TILES + 3):
        rolled[:, c * 128 : (c + 1) * 128] = edge
    pack[192:768, :] = jnp.zeros((576, 128), F32)
    rest[0].wait()

    def tile(c):
        return pl.ds(pl.multiple_of(c * 128, 128), 128)

    @pl.loop(0, TILES)
    def _(c):
        col = c * 128 + lax.broadcasted_iota(jnp.int32, (1, 128), 1)
        mode_a = (col >> 6).astype(F32) * (math.pi / S1)
        mode_b = (col & 63).astype(F32) * (math.pi / S2)
        wave = mode_k + (mode_a * mode_a + mode_b * mode_b)
        slow[:, tile(c)] = jnp.where(own, center, 2.0 - gain[:, tile(c)] * wave)

    rest[1].wait()
    rest[2].wait()
    rest[3].wait()

    def keep_force(force):
        pml = is_pml((PLANE, 128))
        for d in range(3):
            pack[d * 32 : (d + 1) * 32, :] = jnp.where(pml, 0.0, force[d])
            pack[96 + d * 32 : 96 + (d + 1) * 32, :] = jnp.where(pml, 0.0, force[3 + d])
            pack[256 + d * 32 : 256 + (d + 1) * 32, :] = jnp.where(pml, FACE_COEF[d] * force[d], 0.0)
            at = 512 + (7 - d) * 32
            pack[at : at + 32, :] = jnp.where(pml, FACE_COEF[3 + d] * force[3 + d], 0.0)

    def finish(box, table, cut, turn, at, c0, n):
        if n > 0:
            along_box = spread_modes(modes, pack, c0)
            top = both(pack, 256, c0)
            bottom = both(pack, 512, c0)
        for r in range(4):
            row = slice(32 * r, 32 * r + 32)
            for h in range(2):
                here = slice(at + h * 128, at + (h + 1) * 128)
                box_here = slice(at + 128 + h * 128, at + 256 + h * 128)
                turn_here = slice(at + 256 + h * 128, at + 384 + h * 128)
                side = slice(h * 128, (h + 1) * 128)
                block = box[row, box_here]
                if n > 0:
                    block = block + table[row, here] * along_box[row, side]
                    if r == 0:
                        block = jnp.concatenate([block[0:8] + top[:, side], block[8:32]], axis=0)
                    if r == 3:
                        block = jnp.concatenate([block[0:24], block[24:32] + bottom[:, side]], axis=0)
                    box[row, box_here] = block
                hi, lo = split(block)
                cut[row, here] = hi
                cut[slice(128 + 32 * r, 160 + 32 * r), here] = lo
                turn[row, turn_here] = pltpu.roll(block, 64, 1)

    w1, w2 = TAPS_90[0], TAPS_90[1]
    layers_at = jnp.where(lax.rem(gx, 4) == 3, LAYERS_AT[1], LAYERS_AT[0])
    small_first = lax.broadcasted_iota(jnp.int32, (32, 128), 1) < 64

    def keep_taps(cut, at, slot):
        pair = cut[:, at : at + 256]
        operand = jnp.concatenate([stencil[0:128, :], pair[0:128, :], pair[128:256, :]], axis=1)
        fixed = stencil[128:384, :]
        tapped[slot] = dot(operand, jnp.concatenate([pair, fixed, fixed], axis=0))

    def advance(b, p, n):
        def step(base, c0, at, slot, ahead_by, width):
            box = state.at[b, :, pl.ds(base, 256 + width)]
            old = state.at[p, :, pl.ds(base, 256 + width)]
            turn = rolled.at[:, pl.ds(base, 512 + width)]
            cut = halved.at[:, pl.ds(base, width)]
            table = gain.at[:, pl.ds(base, width)]
            own_slow = slow.at[:, pl.ds(base, width)]
            if ahead_by > 0:
                keep_taps(cut, at + 256, 1 - slot)
            if ahead_by > 1:
                finish(box, table, cut, turn, at + 512, c0 + 4, n)
            partial = [None, None]
            ends_ = [[None, None], [None, None]]
            for r in range(4):
                row = slice(32 * r, 32 * r + 32)
                ring = [turn[row, at + i * 128 : at + (i + 1) * 128] for i in range(6)]
                line = [box[row, at + i * 128 : at + (i + 1) * 128] for i in range(4)]
                quads = [w1 * (ring[i + 2] + ring[i + 1]) + (ring[i + 3] + ring[i]) for i in range(3)]
                for h in range(2):
                    here = slice(at + h * 128, at + (h + 1) * 128)
                    box_here = slice(at + 128 + h * 128, at + 256 + h * 128)
                    total = tapped[slot, row, h * 128 : (h + 1) * 128] + w2 * (line[h] + line[h + 2])
                    total += jnp.where(small_first, quads[h], quads[h + 1])
                    following = own_slow[row, here] * line[h + 1]
                    following -= rows[0, row, :] * old[row, box_here]
                    following += rows[1, row, :] * total
                    old[row, box_here] = following
                    partial[h] = face_part(partial[h], following, r)
                    if r == 0:
                        ends_[h][0] = following[0:8]
                    if r == 3:
                        ends_[h][1] = following[24:32]
            for h in range(2):
                note_faces(partial[h], ends_[h][0], ends_[h][1], c0 + h)

        for t in range(2):
            base = t * 256
            finish(
                state.at[b, :, pl.ds(base, 512)], gain.at[:, pl.ds(base, 256)], halved.at[:, pl.ds(base, 256)],
                rolled.at[:, pl.ds(base, 768)], 0, 2 * t, n,
            )
        keep_taps(halved, 0, 0)

        @pl.loop(0, TILES // 4 - 1)
        def _(i):
            base = pl.multiple_of(i * 512, 512)

            @pl.when(jnp.logical_and(ahead_ok, i == FORCES_AT))
            def _():
                pass_forces(n)

            @pl.when(jnp.logical_and(ahead_ok, i == layers_at))
            def _():
                pass_layers(n)

            for s in range(2):
                step(base, 4 * i + 2 * s, 256 * s, s, 2, 1024)

        base = CROSS - 512
        step(base, TILES - 4, 0, 0, 1, 512)
        step(base, TILES - 2, 256, 1, 0, 512)

        for e, plane in enumerate(gathered_faces()):
            free[e * 32 : (e + 1) * 32, :] = plane

    def theirs(r):
        g = jnp.full((8, 128), faces[r, 2], jnp.int32)
        value = jnp.where(g == -1, flag_in[0], jnp.where(g == 0, flag_in[1], flag_in[2]))
        return jnp.broadcast_to(value[0:1, :], (128, 128))

    def finish_matrices():
        for g in (-1, 0, 1):

            @pl.when(jnp.logical_and(ahead_ok, side_ok[g]))
            def _():
                flag_copy(g).wait_recv()

        their = [theirs(r) for r in range(2)]
        their_col = jnp.where(big_col < 64, their[0], their[1]) > 0.5
        cross_one = jnp.where(their_col, one_pml, one_air)
        left[0] = left_form(cross_one)
        left[1] = left_form(cross_one.T)
        for r in range(2):
            cross_two = jnp.where(their[r] > 0.5, two_pml[r], two_air[r])
            right[r] = right_form(cross_two)
            right[2 + r] = right_form(cross_two.T)
        left[2] = left_form(ours_p)
        right[4] = right_form(ours_t)

    unforced = pltpu.make_async_copy(
        state.at[STEPS % 2, :, pl.ds(128, CROSS)], free_out, out_sem.at[0]
    )
    for n in range(STEPS):
        b, p = n % 2, 1 - n % 2
        if n > 0:
            send_back(n)
            make_sums(n)
            send_ahead(n)
            keep_force(force)
        advance(b, p, n)
        if n == 0:
            finish_matrices()
        if n == STEPS - 1:
            unforced.start()
        got_back(n)
        high = high_force(n)
        got_ahead(n)
        low = low_force(n)
        if n == 0:
            turned = dot(stacked(low), right[4])
            low = planes_of(dot(left[2], columns(turned, jnp.zeros((96, 128), F32))), 0)
        else:
            low = [low[e * 32 : (e + 1) * 32, :] for e in range(3)]
        force = low + high
        for e, plane in enumerate(response(force)):
            at = slice(e * 32, (e + 1) * 32)
            layers[n + 1, at, :] = free[at, :] + plane

    keep_force(force)
    pack[768:960, :] = layers[STEPS]
    packed = pltpu.make_async_copy(pack, pack_out, out_sem.at[1])
    packed.start()

    for side, ok in order:

        @pl.when(jnp.logical_and(back_ok, ok))
        def _():
            flag_copy(-side).wait_send()

    @pl.when(back_ok)
    def _():
        for n in range(STEPS):
            low_straight(n, 0).wait_send()
            low_straight(n, 1).wait_send()
            low_other(n).wait_send()

            @pl.when(away_ok)
            def _():
                low_away(n).wait_send()

    @pl.when(ahead_ok)
    def _():
        for n in range(STEPS):
            low_relay(n).wait_send()
            force_pair(n).wait_send()
            force_straight(n).wait_send()

            @pl.when(away_ok)
            def _():
                force_away(n).wait_send()

    unforced.wait()
    packed.wait()


def both(pack, row, c):
    return jnp.concatenate([pack[pl.ds(row + c + h, 8, stride=PLANE), :] for h in range(2)], axis=1)


def spread_modes(modes, pack, c):
    hi, lo = split(both(pack, 0, c))
    hi = hi.astype(F32)
    terms = jnp.concatenate([hi, lo.astype(F32), hi, jnp.zeros((8, 256), F32)], axis=0)
    return dot(modes[...], terms.astype(BF16))


PARTS = 8
WIDE = CROSS // PARTS


def close(flags, pack, misc, free, gain, out, layers_out, done, sems):
    pml = flags[0] > 0
    leave = [
        pltpu.make_async_copy(
            done.at[:, pl.ds(i * WIDE, WIDE)], out.at[0, :, pl.ds(i * WIDE, WIDE)], sems.at[i]
        )
        for i in range(PARTS)
    ]

    @pl.when(pml)
    def _():
        for i in range(PARTS):
            at = slice(i * WIDE, (i + 1) * WIDE)
            done[:, at] = free[:, at]
            for h in range(WIDE // 128):
                c = i * (WIDE // 128) + h
                at = slice(c * 128, (c + 1) * 128)
                done[0:8, at] = free[0:8, at] + pack[pl.ds(256 + c, 8, stride=PLANE), :]
                done[120:128, at] = free[120:128, at] + pack[pl.ds(512 + c, 8, stride=PLANE), :]
            leave[i].start()
        layers_out[...] = pack[768:960, :]

    @pl.when(jnp.logical_not(pml))
    def _():
        even = (lax.broadcasted_iota(jnp.int32, (8, 128), 0) & 1) == 0
        for i in range(PARTS):

            @pl.loop(0, WIDE // 256)
            def _(t):
                window = pl.ds(pl.multiple_of(i * WIDE + t * 256, 256), 256)
                source, table, target = free.at[:, window], gain.at[:, window], done.at[:, window]
                modes = []
                for h in range(2):
                    c = i * (WIDE // 128) + 2 * t + h
                    mode = []
                    for d in range(3):
                        low = jnp.broadcast_to(pack[pl.ds(d * 32 + c, 1), :], (8, 128))
                        high = jnp.broadcast_to(pack[pl.ds(96 + d * 32 + c, 1), :], (8, 128))
                        mode.append(low + jnp.where(even, high, -high))
                    modes.append(mode)
                for r in range(8):
                    row = slice(16 * r, 16 * r + 16)
                    weights = [
                        misc[ROW_FACE + d * 128 + 16 * r : ROW_FACE + d * 128 + 16 * r + 16, :].reshape(2, 8, 128)
                        for d in range(3)
                    ]
                    for h in range(2):
                        at = slice(h * 128, (h + 1) * 128)
                        total = sum(weights[d] * modes[h][d][None] for d in range(3))
                        target[row, at] = source[row, at] + table[row, at] * total.reshape(16, 128)

            leave[i].start()
        turned = dot(stacked(pack[768:960, :]), right_form(misc[ROW_C : ROW_C + 128, :]))
        ours_pt = left_form(misc[ROW_C + 384 : ROW_C + 512, :])
        product = dot(ours_pt, columns(turned[0:96, :], turned[96:192, :]))
        for s in range(2):
            for e, plane in enumerate(planes_of(product, s)):
                at = (3 * s + e) * 32
                layers_out[at : at + 32, :] = plane

    for copy in leave:
        copy.wait()


def local(state_now, state_prev, pml_flags, interfaces):
    gain, misc, stencil, modes = (jnp.asarray(a) for a in constants())
    smem = pl.BlockSpec(memory_space=pltpu.SMEM)
    whole = pl.BlockSpec(memory_space=pltpu.VMEM)
    hbm = pl.BlockSpec(memory_space=pltpu.HBM)
    free, pack = pl.pallas_call(
        exchange,
        out_shape=(
            jax.ShapeDtypeStruct((S0, CROSS), F32),
            jax.ShapeDtypeStruct((960, 128), F32),
        ),
        in_specs=[smem] + [hbm] * 7,
        out_specs=(pl.BlockSpec(memory_space=pl.ANY),) * 2,
        scratch_shapes=[
            pltpu.VMEM((2, S0, CROSS + 256), F32),
            pltpu.VMEM((S0, CROSS), F32),
            pltpu.VMEM((S0, CROSS), F32),
            pltpu.VMEM(misc.shape, F32),
            pltpu.VMEM(modes.shape, BF16),
            pltpu.VMEM(stencil.shape, BF16),
            pltpu.VMEM((256, CROSS), BF16),
            pltpu.VMEM((S0, CROSS + 512), F32),
            pltpu.VMEM((2, 128, 256), F32),
            pltpu.VMEM((2, 128, 128), F32),
            pltpu.VMEM((256, 128), F32),
            pltpu.VMEM((256, 128), F32),
            pltpu.VMEM((192, 128), F32),
            pltpu.VMEM((3, 128, 384), BF16),
            pltpu.VMEM((5, 384, 128), BF16),
            pltpu.VMEM((8, 128), F32),
            pltpu.VMEM((3, 8, 128), F32),
            pltpu.VMEM((STEPS + 1, 192, 128), F32),
            pltpu.VMEM((STEPS, 4, 96, 128), F32),
            pltpu.VMEM((STEPS, 3, 96, 128), F32),
            pltpu.VMEM((STEPS, 3, 96, 128), F32),
            pltpu.VMEM((STEPS, 96, 128), F32),
            pltpu.VMEM((960, 128), F32),
            pltpu.SMEM((2, 6), jnp.int32),
            pltpu.SemaphoreType.DMA((10,)),
            pltpu.SemaphoreType.DMA((27,)),
            pltpu.SemaphoreType.DMA((27,)),
            pltpu.SemaphoreType.DMA((2,)),
        ],
        compiler_params=pltpu.CompilerParams(
            collective_id=0, has_side_effects=True, vmem_limit_bytes=32 * 1024 * 1024
        ),
    )(
        pml_flags,
        *(
            pltpu.with_memory_space_constraint(x, pltpu.HBM)
            for x in (interfaces, state_now, state_prev, gain, misc, stencil, modes)
        ),
    )

    new_state, planes = pl.pallas_call(
        close,
        out_shape=(
            jax.ShapeDtypeStruct((1, S0, CROSS), F32),
            jax.ShapeDtypeStruct((192, 128), F32),
        ),
        in_specs=[smem] + [whole] * 4,
        out_specs=(hbm, whole),
        scratch_shapes=[pltpu.VMEM((S0, CROSS), F32), pltpu.SemaphoreType.DMA((PARTS,))],
        compiler_params=pltpu.CompilerParams(vmem_limit_bytes=24 * 1024 * 1024),
    )(pml_flags, pack, misc, free, gain)
    return new_state, planes.reshape(1, 6, CROSS)


def solution(mesh):
    one, two, three = P(("gx", "gy")), P(("gx", "gy"), None), P(("gx", "gy"), None, None)
    return jax.shard_map(
        local,
        mesh=mesh,
        in_specs=(three, three, one, two),
        out_specs=(three, three),
        check_vma=False,
    )
```

```python
import math

import jax
import jax.numpy as jnp
import numpy as np
from jax import lax
from jax.experimental import pallas as pl
from jax.experimental.pallas import tpu as pltpu
from jax.sharding import PartitionSpec as P

S0 = 128
S1 = 64
S2 = 64
CROSS = S1 * S2
STEPS = 3
FORCES_AT = 1
LAYERS_AT = (4, 6)
TILES = CROSS // 128
PLANE = 32
MESH = pl.DeviceIdType.MESH
F32 = jnp.float32
BF16 = jnp.bfloat16

COURANT2 = 0.16
CENTER3 = 3.0 * (-490.0 / 180.0)
TAPS = (1.5, -0.15, 1.0 / 90.0)
TAPS_90 = (135.0, -13.5, 1.0)
PAIRS = {(0, 0): 0, (0, 1): 1, (0, 2): 2, (1, 1): 3, (1, 2): 4, (2, 2): 5}


def basis(n):
    k = np.arange(n)[:, None]
    i = np.arange(n)[None, :]
    weight = np.where(k == 0, math.sqrt(1.0 / n), math.sqrt(2.0 / n))
    return weight * np.cos(math.pi * k * (i + 0.5) / n)


def twice(a):
    n = a.shape[0]
    out = np.zeros((2 * n, 2 * n))
    out[:n, :n] = a
    out[n:, n:] = a
    return out


def constants():
    c0, c1 = basis(S0), basis(S1)
    k = (math.pi * np.arange(S0) / S0) ** 2
    a = (math.pi * np.arange(S1) / S1) ** 2
    wave = (k[:, None, None] + a[None, :, None] + a[None, None, :]).reshape(S0, CROSS)
    safe = np.where(wave > 0, wave, 1.0)
    gain = np.where(wave > 0, 4.0 * np.sin(0.2 * np.sqrt(wave)) ** 2 / safe, COURANT2)
    face = c0[:, :3]
    sign = (-1.0) ** np.arange(S0)
    planes = []
    for s in (np.ones(S0), sign):
        for d, e in PAIRS:
            planes.append(((face[:, d] * face[:, e] * s) @ gain).reshape(PLANE, 128))
    order = np.concatenate([np.arange(0, S1, 2), np.arange(1, S1, 2)])
    c1p = c1[order][:, order]
    misc = np.concatenate(
        [np.repeat(face[:, d : d + 1], 128, axis=1) for d in range(3)]
        + planes
        + [twice(c1), twice(c1.T), twice(c1p), twice(c1p.T)],
        axis=0,
    )

    def band(n):
        out = np.zeros((n, n))
        for distance, tap in enumerate(TAPS_90, 1):
            out += tap * (np.eye(n, k=distance) + np.eye(n, k=-distance))
        return out

    along = band(S0)
    stencil = np.concatenate([np.concatenate([along, along], axis=1), twice(twice(band(S2)))], axis=0)
    six = np.zeros((S0, 8))
    six[:, 0:6] = c0[:, [0, 1, 2, 127, 126, 125]]
    high = six.astype(np.float32).astype(BF16)
    low = (six - high.astype(np.float64)).astype(np.float32).astype(BF16)
    modes = np.concatenate([high, high, low, np.zeros((S0, 8), BF16)], axis=1)
    return gain.astype(np.float32), misc.astype(np.float32), stencil.astype(BF16), modes


ROW_FACE, ROW_P, ROW_C = 0, 384, 768


def rate_of(row):
    return 0.5 * ((row + 0.5) / S0) ** 2


FACE_COEF = [COURANT2 / (1.0 + rate_of(i)) for i in (0, 1, 2, 127, 126, 125)]


def split(x):
    high = x.astype(BF16)
    return high, (x - high.astype(F32)).astype(BF16)


def dot(a, b):
    return jnp.dot(a, b, preferred_element_type=F32)


def couple(p):
    w1, w2, w3 = TAPS
    return [w1 * p[0] + w2 * p[1] + w3 * p[2], w2 * p[0] + w3 * p[1], w3 * p[0]]


def stacked(x):
    hi, lo = split(x)
    return jnp.concatenate([hi, lo, hi], axis=1)


def first_half():
    return lax.broadcasted_iota(jnp.int32, (PLANE, 128), 1) < 64


def columns(*sets):
    first = first_half()
    outer = []
    for w in sets:
        even, odd = [], []
        for e in range(3):
            p = w[e * 32 : (e + 1) * 32, :]
            swapped = pltpu.roll(p, 64, 1)
            even.append(jnp.where(first, p, swapped))
            odd.append(jnp.where(first, swapped, p))
        outer.append(jnp.concatenate(even, axis=1))
        outer.append(jnp.concatenate(odd, axis=1))
    hi, lo = split(jnp.concatenate(outer, axis=0))
    return jnp.concatenate([hi, lo, hi], axis=0)


def planes_of(product, s):
    first = first_half()
    top = product[64 * s : 64 * s + 32, :]
    bottom = product[64 * s + 32 : 64 * s + 64, :]
    return [
        jnp.where(first, top[:, e * 128 : (e + 1) * 128], bottom[:, e * 128 : (e + 1) * 128])
        for e in range(3)
    ]


def left_form(matrix):
    hi, lo = split(matrix)
    return jnp.concatenate([hi, hi, lo], axis=1)


def right_form(matrix):
    hi, lo = split(matrix)
    return jnp.concatenate([hi, hi, lo], axis=0)


def exchange(
    flags, faces_hbm, now_hbm, prev_hbm, gain_hbm, misc_hbm, stencil_hbm, modes_hbm,
    free_out, pack_out,
    state, gain, slow, misc, modes, stencil, halved, rolled, tapped, rows,
    acc, picked, free, left, right, flag_out, flag_in, layers, sums, low_in, force_in, pair_in, pack,
    faces, load_sem, send_sem, recv_sem, out_sem,
):
    gx, gy = lax.axis_index("gx"), lax.axis_index("gy")
    nx, ny = lax.axis_size("gx"), lax.axis_size("gy")

    def table(first, last, sem):
        at = pl.ds(first, last - first)
        return pltpu.make_async_copy(misc_hbm.at[at], misc.at[at], load_sem.at[sem])

    head = table(ROW_C, ROW_C + 512, 0)
    head.start()
    weights_load = table(ROW_FACE, ROW_P, 10)
    weights_load.start()
    listed = pltpu.make_async_copy(faces_hbm, faces, load_sem.at[8])
    listed.start()
    chunk = CROSS // 4
    nows = [
        pltpu.make_async_copy(
            now_hbm.at[0, :, pl.ds(i * chunk, chunk)],
            state.at[0, :, pl.ds(128 + i * chunk, chunk)],
            load_sem.at[4 + i],
        )
        for i in range(4)
    ]
    for load in nows:
        load.start()
    rest = [
        pltpu.make_async_copy(gain_hbm, gain, load_sem.at[1]),
        pltpu.make_async_copy(prev_hbm.at[0], state.at[1, :, pl.ds(128, CROSS)], load_sem.at[2]),
        pltpu.make_async_copy(stencil_hbm, stencil, load_sem.at[3]),
        pltpu.make_async_copy(modes_hbm, modes, load_sem.at[9]),
        table(ROW_P, ROW_C, 11),
    ]
    for load in rest:
        load.start()
    core = lax.rem(gy, 2)
    away = 2 * core - 1
    other = -away
    away_ok = jnp.where(core == 0, gy > 0, gy < ny - 1)
    order = ((away, away_ok), (other, gy >= 0), (0, gy >= 0))

    back_ok, ahead_ok = gx > 0, gx < nx - 1
    side_ok = {-1: gy > 0, 0: gy >= 0, 1: gy < ny - 1}
    barrier = pltpu.get_barrier_semaphore()
    for ok, to_x in ((back_ok, gx - 1), (ahead_ok, gx + 1)):
        for side in (-1, 0, 1):

            @pl.when(jnp.logical_and(ok, side_ok[side]))
            def _():
                pl.semaphore_signal(barrier, inc=1, device_id=(to_x, gy + side), device_id_type=MESH)

    pl.semaphore_signal(barrier, inc=1, device_id=(gx, gy + other), device_id_type=MESH)
    flag_out[...] = jnp.full(flag_out.shape, flags[0], jnp.int32).astype(F32)

    def send(source, target, sem, to_x, to_y):
        return pltpu.make_async_remote_copy(
            src_ref=source, dst_ref=target, send_sem=send_sem.at[sem], recv_sem=recv_sem.at[sem],
            device_id=(to_x, to_y), device_id_type=MESH,
        )

    def flag_copy(g):
        return send(flag_out, flag_in.at[g + 1], g + 1, gx - 1, gy - g)

    half = (pl.ds(0, 48), pl.ds(48, 48))

    def low_straight(n, h):
        return send(layers.at[n, half[h]], low_in.at[n, 1, half[h]], 3 + 8 * n + h, gx - 1, gy)

    def low_away(n):
        return send(layers.at[n, pl.ds(0, 96)], low_in.at[n, 1 - away], 5 + 8 * n, gx - 1, gy + away)

    def low_other(n):
        return send(layers.at[n, half[0]], low_in.at[n, 1 - other, half[0]], 6 + 8 * n, gx - 1, gy + other)

    def low_relay(n):
        return send(low_in.at[n, 1, half[1]], low_in.at[n, 1 - other, half[1]], 7 + 8 * n, gx, gy + other)

    def force_away(n):
        return send(sums.at[n, away + 1], force_in.at[n, away + 1], 8 + 8 * n, gx + 1, gy + away)

    def force_pair(n):
        return send(sums.at[n, other + 1], pair_in.at[n], 9 + 8 * n, gx, gy + other)

    def force_straight(n):
        return send(sums.at[n, 3], force_in.at[n, 1], 10 + 8 * n, gx + 1, gy)

    def send_back(n):
        @pl.when(back_ok)
        def _():
            low_straight(n, 1).start()

            @pl.when(away_ok)
            def _():
                low_away(n).start()

            low_straight(n, 0).start()
            low_other(n).start()

    def send_ahead(n):
        @pl.when(ahead_ok)
        def _():
            force_pair(n).start()

            @pl.when(away_ok)
            def _():
                force_away(n).start()

    def pass_forces(n):
        force_pair(n).wait_recv()
        sums[n, 3] = sums[n, 1] + pair_in[n]
        force_straight(n).start()

    def pass_layers(n):
        low_straight(n, 1).wait_recv()
        low_relay(n).start()

    def got_back(n):
        @pl.when(ahead_ok)
        def _():
            low_straight(n, 0).wait_recv()
            low_other(n).wait_recv()
            low_relay(n).wait_recv()

            @pl.when(away_ok)
            def _():
                low_away(n).wait_recv()

    def got_ahead(n):
        @pl.when(back_ok)
        def _():
            force_straight(n).wait_recv()

            @pl.when(away_ok)
            def _():
                force_away(n).wait_recv()

    def is_pml(shape):
        return jnp.full(shape, flags[0], jnp.int32) > 0

    listed.wait()
    head.wait()
    big_row = lax.broadcasted_iota(jnp.int32, (128, 128), 0)
    big_col = lax.broadcasted_iota(jnp.int32, (128, 128), 1)
    same = (big_row >> 6) == (big_col >> 6)
    eye = jnp.where(big_row == big_col, 1.0, 0.0).astype(F32)
    own = is_pml((128, 128))
    basis_c, basis_ct, basis_p, basis_pt = (
        misc[ROW_C + i * 128 : ROW_C + (i + 1) * 128, :] for i in range(4)
    )
    ours, ours_t, ours_p, ours_pt = (
        jnp.where(own, eye, m) for m in (basis_c, basis_ct, basis_p, basis_pt)
    )
    q_row, q_col = big_row & 63, big_col & 63
    j_row = 2 * (q_row & 31) + (q_row >> 5)
    j_col = 2 * (q_col & 31) + (q_col >> 5)
    upper = big_row < 64
    step_one = jnp.where(
        upper,
        jnp.full((128, 128), faces[0, 3], jnp.int32),
        jnp.full((128, 128), faces[1, 3], jnp.int32),
    )

    def one_hot(where):
        return jnp.where(where, 1.0, 0.0).astype(BF16)

    def by_exact(a, b):
        hi, lo = split(a)
        return dot(jnp.concatenate([hi, lo], axis=1), jnp.concatenate([b, b], axis=0))

    def exact_by(a, b):
        hi, lo = split(b)
        return dot(jnp.concatenate([a, a], axis=1), jnp.concatenate([hi, lo], axis=0))

    one_pml = by_exact(ours_p, one_hot(jnp.logical_and(same, j_col == j_row - step_one)))
    one_air = dot(stacked(one_pml), right_form(basis_pt))
    two_pml, two_air = [], []
    for r in range(2):
        step_two = jnp.full((128, 128), faces[r, 4], jnp.int32)
        two_pml.append(exact_by(one_hot(jnp.logical_and(same, q_row == q_col - step_two)), ours_t))
        two_air.append(dot(stacked(basis_c), right_form(two_pml[r])))

    left[1] = left_form(one_pml.T)
    right[2] = right_form(two_pml[0].T)
    right[3] = right_form(two_pml[1].T)

    sides = 1 + (gy > 0).astype(jnp.int32) + (gy < ny - 1).astype(jnp.int32)
    ends = (gx > 0).astype(jnp.int32) + (gx < nx - 1).astype(jnp.int32)
    pl.semaphore_wait(barrier, sides * ends + 1)
    for side, ok in order:

        @pl.when(jnp.logical_and(back_ok, ok))
        def _():
            flag_copy(-side).start()


    line = lax.broadcasted_iota(jnp.int32, (8, 128), 0)

    def note_faces(partial, top, bottom, c):
        full = []
        for d in range(3):
            v = partial[d] + pltpu.roll(partial[d], 4, 0)
            full.append(v + pltpu.roll(v, 2, 0))
        at = pl.ds(pl.multiple_of(c * 8, 8), 8)
        acc[at, :] = jnp.where(line < 2, full[0], jnp.where(line < 4, full[1], full[2]))
        picked[at, :] = jnp.where(line < 4, top, bottom)

    def face_part(partial, chunk_rows, r):
        tiles = chunk_rows.reshape(4, 8, 128)
        out = []
        for d in range(3):
            at = ROW_FACE + d * 128 + 32 * r
            weights = misc[at : at + 32, :].reshape(4, 8, 128)
            term = jnp.sum(weights * tiles, axis=0)
            out.append(term if partial is None else partial[d] + term)
        return out

    def gathered_faces():
        low, high = [], []
        pml = is_pml((PLANE, 128))
        for d in range(3):
            even = acc[pl.ds(2 * d, PLANE, stride=8), :]
            odd = acc[pl.ds(2 * d + 1, PLANE, stride=8), :]
            row_low = picked[pl.ds(d, PLANE, stride=8), :]
            row_high = picked[pl.ds(7 - d, PLANE, stride=8), :]
            low.append(jnp.where(pml, row_low, even + odd))
            high.append(jnp.where(pml, row_high, even - odd))
        return low + high

    weights_load.wait()
    for i in range(4):
        nows[i].wait()

        @pl.loop(0, TILES // 8)
        def _(t):
            window = state.at[0, :, pl.ds(pl.multiple_of(128 + i * chunk + t * 256, 128), 256)]
            ats = [slice(h * 128, (h + 1) * 128) for h in range(2)]
            partial = [None, None]
            for r in range(4):
                for h in range(2):
                    partial[h] = face_part(partial[h], window[32 * r : 32 * r + 32, ats[h]], r)
            for h in range(2):
                note_faces(partial[h], window[0:8, ats[h]], window[120:128, ats[h]], 8 * i + 2 * t + h)

    for e, plane in enumerate(gathered_faces()):
        layers[0, e * 32 : (e + 1) * 32, :] = plane
    send_back(0)

    def chosen(r, g):
        return jnp.logical_and(
            jnp.full((96, 128), faces[r, 2], jnp.int32) == g,
            jnp.full((96, 128), faces[r, 5], jnp.int32) > 0,
        )

    def make_sums(n):
        z = couple([layers[n, (3 + d) * 32 : (4 + d) * 32, :] for d in range(3)])
        z3 = stacked(jnp.concatenate(z, axis=0))
        product = dot(left[1], columns(dot(z3, right[2]), dot(z3, right[3])))
        moved = [jnp.concatenate(planes_of(product, r), axis=0) for r in range(2)]
        for g in (-1, 0, 1):
            total = jnp.where(chosen(0, g), moved[0], 0.0) + jnp.where(chosen(1, g), moved[1], 0.0)
            sums[n, g + 1] = total

    def high_force(n):
        parts = []
        for r in range(2):
            pick = jnp.zeros((96, 128), F32)
            for g in (-1, 0, 1):
                pick = jnp.where(chosen(r, g), low_in[n, g + 1], pick)
            parts.append(dot(stacked(pick), right[r]))
        product = dot(left[0], columns(parts[0], parts[1]))
        a, b = planes_of(product, 0), planes_of(product, 1)
        return couple([x + y for x, y in zip(a, b)])

    def low_force(n):
        straight_there = jnp.full((96, 128), back_ok.astype(jnp.int32), jnp.int32) > 0
        away_there = jnp.full((96, 128), jnp.logical_and(back_ok, away_ok).astype(jnp.int32), jnp.int32) > 0
        total = jnp.where(straight_there, force_in[n, 1], 0.0)
        total += jnp.where(away_there, force_in[n, 1 - away], 0.0)
        return total

    def response(force):
        pml = is_pml((PLANE, 128))
        low, high = [], []
        for d in range(3):
            near, far = 0.0, 0.0
            for e in range(3):
                i = PAIRS[(min(d, e), max(d, e))]
                p = misc[ROW_P + i * 32 : ROW_P + (i + 1) * 32, :]
                q = misc[ROW_P + 192 + i * 32 : ROW_P + 192 + (i + 1) * 32, :]
                near = near + (p * force[e] + q * force[3 + e])
                far = far + (q * force[e] + p * force[3 + e])
            low.append(jnp.where(pml, FACE_COEF[d] * force[d], near))
            high.append(jnp.where(pml, FACE_COEF[3 + d] * force[3 + d], far))
        return low + high

    make_sums(0)
    send_ahead(0)
    k = big_row.astype(F32)
    rate = 0.5 * ((k + 0.5) * (1.0 / S0)) ** 2
    inverse = 1.0 / (1.0 + rate)
    rows[0] = jnp.where(own, (1.0 - rate) * inverse, 1.0)
    rows[1] = jnp.where(own, (COURANT2 / 90.0) * inverse, 0.0)
    center = (2.0 + COURANT2 * CENTER3) * inverse
    mode_k = (k * (math.pi / S0)) * (k * (math.pi / S0))
    edge = jnp.zeros((S0, 128), F32)
    for b in range(2):
        state[b, :, 0:128] = edge
        state[b, :, 128 + CROSS : 256 + CROSS] = edge
    for c in (0, 1, TILES + 2, TILES + 3):
        rolled[:, c * 128 : (c + 1) * 128] = edge
    pack[192:768, :] = jnp.zeros((576, 128), F32)
    rows[2] = center
    rows[3] = mode_k
    rest[0].wait()

    def tile(c):
        return pl.ds(pl.multiple_of(c * 128, 128), 128)

    rest[1].wait()
    rest[2].wait()
    rest[3].wait()
    rest[4].wait()

    def keep_force(force):
        pml = is_pml((PLANE, 128))
        for d in range(3):
            pack[d * 32 : (d + 1) * 32, :] = jnp.where(pml, 0.0, force[d])
            pack[96 + d * 32 : 96 + (d + 1) * 32, :] = jnp.where(pml, 0.0, force[3 + d])
            pack[256 + d * 32 : 256 + (d + 1) * 32, :] = jnp.where(pml, FACE_COEF[d] * force[d], 0.0)
            at = 512 + (7 - d) * 32
            pack[at : at + 32, :] = jnp.where(pml, FACE_COEF[3 + d] * force[3 + d], 0.0)

    def finish(box, table, cut, turn, at, c0, n):
        if n > 0:
            along_box = spread_modes(modes, pack, c0)
            top = both(pack, 256, c0)
            bottom = both(pack, 512, c0)
        for r in range(4):
            row = slice(32 * r, 32 * r + 32)
            for h in range(2):
                here = slice(at + h * 128, at + (h + 1) * 128)
                box_here = slice(at + 128 + h * 128, at + 256 + h * 128)
                turn_here = slice(at + 256 + h * 128, at + 384 + h * 128)
                side = slice(h * 128, (h + 1) * 128)
                block = box[row, box_here]
                if n > 0:
                    block = block + table[row, here] * along_box[row, side]
                    if r == 0:
                        block = jnp.concatenate([block[0:8] + top[:, side], block[8:32]], axis=0)
                    if r == 3:
                        block = jnp.concatenate([block[0:24], block[24:32] + bottom[:, side]], axis=0)
                    box[row, box_here] = block
                hi, lo = split(block)
                cut[row, here] = hi
                cut[slice(128 + 32 * r, 160 + 32 * r), here] = lo
                turn[row, turn_here] = pltpu.roll(block, 64, 1)

    w1, w2 = TAPS_90[0], TAPS_90[1]
    layers_at = jnp.where(lax.rem(gx, 4) == 3, LAYERS_AT[1], LAYERS_AT[0])
    small_first = lax.broadcasted_iota(jnp.int32, (32, 128), 1) < 64

    def keep_taps(cut, at, slot):
        pair = cut[:, at : at + 256]
        operand = jnp.concatenate([stencil[0:128, :], pair[0:128, :], pair[128:256, :]], axis=1)
        fixed = stencil[128:384, :]
        tapped[slot] = dot(operand, jnp.concatenate([pair, fixed, fixed], axis=0))

    def advance(b, p, n):
        def step(base, c0, at, slot, ahead_by, width):
            box = state.at[b, :, pl.ds(base, 256 + width)]
            old = state.at[p, :, pl.ds(base, 256 + width)]
            turn = rolled.at[:, pl.ds(base, 512 + width)]
            cut = halved.at[:, pl.ds(base, width)]
            table = gain.at[:, pl.ds(base, width)]
            own_slow = slow.at[:, pl.ds(base, width)]
            if ahead_by > 0:
                keep_taps(cut, at + 256, 1 - slot)
            if ahead_by > 1:
                finish(box, table, cut, turn, at + 512, c0 + 4, n)
            partial = [None, None]
            ends_ = [[None, None], [None, None]]
            for r in range(4):
                row = slice(32 * r, 32 * r + 32)
                ring = [turn[row, at + i * 128 : at + (i + 1) * 128] for i in range(6)]
                line = [box[row, at + i * 128 : at + (i + 1) * 128] for i in range(4)]
                quads = [w1 * (ring[i + 2] + ring[i + 1]) + (ring[i + 3] + ring[i]) for i in range(3)]
                for h in range(2):
                    here = slice(at + h * 128, at + (h + 1) * 128)
                    box_here = slice(at + 128 + h * 128, at + 256 + h * 128)
                    total = tapped[slot, row, h * 128 : (h + 1) * 128] + w2 * (line[h] + line[h + 2])
                    total += jnp.where(small_first, quads[h], quads[h + 1])
                    if n == 0:
                        col = (c0 + h) * 128 + lax.broadcasted_iota(jnp.int32, (1, 128), 1)
                        mode_a = (col >> 6).astype(F32) * (math.pi / S1)
                        mode_b = (col & 63).astype(F32) * (math.pi / S2)
                        wave = rows[3, row, :] + (mode_a * mode_a + mode_b * mode_b)
                        doubled = 2.0 - table[row, here] * wave
                        own_slow[row, here] = jnp.where(is_pml((32, 128)), rows[2, row, :], doubled)
                    following = own_slow[row, here] * line[h + 1]
                    following -= rows[0, row, :] * old[row, box_here]
                    following += rows[1, row, :] * total
                    old[row, box_here] = following
                    partial[h] = face_part(partial[h], following, r)
                    if r == 0:
                        ends_[h][0] = following[0:8]
                    if r == 3:
                        ends_[h][1] = following[24:32]
            for h in range(2):
                note_faces(partial[h], ends_[h][0], ends_[h][1], c0 + h)

        for t in range(2):
            base = t * 256
            finish(
                state.at[b, :, pl.ds(base, 512)], gain.at[:, pl.ds(base, 256)], halved.at[:, pl.ds(base, 256)],
                rolled.at[:, pl.ds(base, 768)], 0, 2 * t, n,
            )
        keep_taps(halved, 0, 0)

        @pl.loop(0, TILES // 4 - 1)
        def _(i):
            base = pl.multiple_of(i * 512, 512)

            @pl.when(jnp.logical_and(ahead_ok, i == FORCES_AT))
            def _():
                pass_forces(n)

            @pl.when(jnp.logical_and(ahead_ok, i == layers_at))
            def _():
                pass_layers(n)

            for s in range(2):
                step(base, 4 * i + 2 * s, 256 * s, s, 2, 1024)

        base = CROSS - 512
        step(base, TILES - 4, 0, 0, 1, 512)
        step(base, TILES - 2, 256, 1, 0, 512)

        for e, plane in enumerate(gathered_faces()):
            free[e * 32 : (e + 1) * 32, :] = plane

    def theirs(r):
        g = jnp.full((8, 128), faces[r, 2], jnp.int32)
        value = jnp.where(g == -1, flag_in[0], jnp.where(g == 0, flag_in[1], flag_in[2]))
        return jnp.broadcast_to(value[0:1, :], (128, 128))

    def finish_matrices():
        for g in (-1, 0, 1):

            @pl.when(jnp.logical_and(ahead_ok, side_ok[g]))
            def _():
                flag_copy(g).wait_recv()

        their = [theirs(r) for r in range(2)]
        their_col = jnp.where(big_col < 64, their[0], their[1]) > 0.5
        cross_one = jnp.where(their_col, one_pml, one_air)
        left[0] = left_form(cross_one)
        left[1] = left_form(cross_one.T)
        for r in range(2):
            cross_two = jnp.where(their[r] > 0.5, two_pml[r], two_air[r])
            right[r] = right_form(cross_two)
            right[2 + r] = right_form(cross_two.T)
        left[2] = left_form(ours_p)
        right[4] = right_form(ours_t)

    unforced = pltpu.make_async_copy(
        state.at[STEPS % 2, :, pl.ds(128, CROSS)], free_out, out_sem.at[0]
    )
    for n in range(STEPS):
        b, p = n % 2, 1 - n % 2
        if n > 0:
            send_back(n)
            make_sums(n)
            send_ahead(n)
            keep_force(force)
        advance(b, p, n)
        if n == 0:
            finish_matrices()
        if n == STEPS - 1:
            unforced.start()
        got_back(n)
        high = high_force(n)
        got_ahead(n)
        low = low_force(n)
        if n == 0:
            turned = dot(stacked(low), right[4])
            low = planes_of(dot(left[2], columns(turned, jnp.zeros((96, 128), F32))), 0)
        else:
            low = [low[e * 32 : (e + 1) * 32, :] for e in range(3)]
        force = low + high
        for e, plane in enumerate(response(force)):
            at = slice(e * 32, (e + 1) * 32)
            layers[n + 1, at, :] = free[at, :] + plane

    keep_force(force)
    pack[768:960, :] = layers[STEPS]
    packed = pltpu.make_async_copy(pack, pack_out, out_sem.at[1])
    packed.start()

    for side, ok in order:

        @pl.when(jnp.logical_and(back_ok, ok))
        def _():
            flag_copy(-side).wait_send()

    @pl.when(back_ok)
    def _():
        for n in range(STEPS):
            low_straight(n, 0).wait_send()
            low_straight(n, 1).wait_send()
            low_other(n).wait_send()

            @pl.when(away_ok)
            def _():
                low_away(n).wait_send()

    @pl.when(ahead_ok)
    def _():
        for n in range(STEPS):
            low_relay(n).wait_send()
            force_pair(n).wait_send()
            force_straight(n).wait_send()

            @pl.when(away_ok)
            def _():
                force_away(n).wait_send()

    unforced.wait()
    packed.wait()


def both(pack, row, c):
    return jnp.concatenate([pack[pl.ds(row + c + h, 8, stride=PLANE), :] for h in range(2)], axis=1)


def spread_modes(modes, pack, c):
    hi, lo = split(both(pack, 0, c))
    hi = hi.astype(F32)
    terms = jnp.concatenate([hi, lo.astype(F32), hi, jnp.zeros((8, 256), F32)], axis=0)
    return dot(modes[...], terms.astype(BF16))


PARTS = 8
WIDE = CROSS // PARTS


def close(flags, pack, misc, free, gain, out, layers_out, done, sems):
    pml = flags[0] > 0
    leave = [
        pltpu.make_async_copy(
            done.at[:, pl.ds(i * WIDE, WIDE)], out.at[0, :, pl.ds(i * WIDE, WIDE)], sems.at[i]
        )
        for i in range(PARTS)
    ]

    @pl.when(pml)
    def _():
        for i in range(PARTS):
            at = slice(i * WIDE, (i + 1) * WIDE)
            done[:, at] = free[:, at]
            for h in range(WIDE // 128):
                c = i * (WIDE // 128) + h
                at = slice(c * 128, (c + 1) * 128)
                done[0:8, at] = free[0:8, at] + pack[pl.ds(256 + c, 8, stride=PLANE), :]
                done[120:128, at] = free[120:128, at] + pack[pl.ds(512 + c, 8, stride=PLANE), :]
            leave[i].start()
        layers_out[...] = pack[768:960, :]

    @pl.when(jnp.logical_not(pml))
    def _():
        even = (lax.broadcasted_iota(jnp.int32, (8, 128), 0) & 1) == 0
        for i in range(PARTS):

            @pl.loop(0, WIDE // 256)
            def _(t):
                window = pl.ds(pl.multiple_of(i * WIDE + t * 256, 256), 256)
                source, table, target = free.at[:, window], gain.at[:, window], done.at[:, window]
                modes = []
                for h in range(2):
                    c = i * (WIDE // 128) + 2 * t + h
                    mode = []
                    for d in range(3):
                        low = jnp.broadcast_to(pack[pl.ds(d * 32 + c, 1), :], (8, 128))
                        high = jnp.broadcast_to(pack[pl.ds(96 + d * 32 + c, 1), :], (8, 128))
                        mode.append(low + jnp.where(even, high, -high))
                    modes.append(mode)
                for r in range(8):
                    row = slice(16 * r, 16 * r + 16)
                    weights = [
                        misc[ROW_FACE + d * 128 + 16 * r : ROW_FACE + d * 128 + 16 * r + 16, :].reshape(2, 8, 128)
                        for d in range(3)
                    ]
                    for h in range(2):
                        at = slice(h * 128, (h + 1) * 128)
                        total = sum(weights[d] * modes[h][d][None] for d in range(3))
                        target[row, at] = source[row, at] + table[row, at] * total.reshape(16, 128)

            leave[i].start()
        turned = dot(stacked(pack[768:960, :]), right_form(misc[ROW_C : ROW_C + 128, :]))
        ours_pt = left_form(misc[ROW_C + 384 : ROW_C + 512, :])
        product = dot(ours_pt, columns(turned[0:96, :], turned[96:192, :]))
        for s in range(2):
            for e, plane in enumerate(planes_of(product, s)):
                at = (3 * s + e) * 32
                layers_out[at : at + 32, :] = plane

    for copy in leave:
        copy.wait()


def local(state_now, state_prev, pml_flags, interfaces):
    gain, misc, stencil, modes = (jnp.asarray(a) for a in constants())
    smem = pl.BlockSpec(memory_space=pltpu.SMEM)
    whole = pl.BlockSpec(memory_space=pltpu.VMEM)
    hbm = pl.BlockSpec(memory_space=pltpu.HBM)
    free, pack = pl.pallas_call(
        exchange,
        out_shape=(
            jax.ShapeDtypeStruct((S0, CROSS), F32),
            jax.ShapeDtypeStruct((960, 128), F32),
        ),
        in_specs=[smem] + [hbm] * 7,
        out_specs=(pl.BlockSpec(memory_space=pl.ANY),) * 2,
        scratch_shapes=[
            pltpu.VMEM((2, S0, CROSS + 256), F32),
            pltpu.VMEM((S0, CROSS), F32),
            pltpu.VMEM((S0, CROSS), F32),
            pltpu.VMEM(misc.shape, F32),
            pltpu.VMEM(modes.shape, BF16),
            pltpu.VMEM(stencil.shape, BF16),
            pltpu.VMEM((256, CROSS), BF16),
            pltpu.VMEM((S0, CROSS + 512), F32),
            pltpu.VMEM((2, 128, 256), F32),
            pltpu.VMEM((4, 128, 128), F32),
            pltpu.VMEM((256, 128), F32),
            pltpu.VMEM((256, 128), F32),
            pltpu.VMEM((192, 128), F32),
            pltpu.VMEM((3, 128, 384), BF16),
            pltpu.VMEM((5, 384, 128), BF16),
            pltpu.VMEM((8, 128), F32),
            pltpu.VMEM((3, 8, 128), F32),
            pltpu.VMEM((STEPS + 1, 192, 128), F32),
            pltpu.VMEM((STEPS, 4, 96, 128), F32),
            pltpu.VMEM((STEPS, 3, 96, 128), F32),
            pltpu.VMEM((STEPS, 3, 96, 128), F32),
            pltpu.VMEM((STEPS, 96, 128), F32),
            pltpu.VMEM((960, 128), F32),
            pltpu.SMEM((2, 6), jnp.int32),
            pltpu.SemaphoreType.DMA((12,)),
            pltpu.SemaphoreType.DMA((27,)),
            pltpu.SemaphoreType.DMA((27,)),
            pltpu.SemaphoreType.DMA((2,)),
        ],
        compiler_params=pltpu.CompilerParams(
            collective_id=0, has_side_effects=True, vmem_limit_bytes=32 * 1024 * 1024
        ),
    )(
        pml_flags,
        *(
            pltpu.with_memory_space_constraint(x, pltpu.HBM)
            for x in (interfaces, state_now, state_prev, gain, misc, stencil, modes)
        ),
    )

    new_state, planes = pl.pallas_call(
        close,
        out_shape=(
            jax.ShapeDtypeStruct((1, S0, CROSS), F32),
            jax.ShapeDtypeStruct((192, 128), F32),
        ),
        in_specs=[smem] + [whole] * 4,
        out_specs=(hbm, whole),
        scratch_shapes=[pltpu.VMEM((S0, CROSS), F32), pltpu.SemaphoreType.DMA((PARTS,))],
        compiler_params=pltpu.CompilerParams(vmem_limit_bytes=24 * 1024 * 1024),
    )(pml_flags, pack, misc, free, gain)
    return new_state, planes.reshape(1, 6, CROSS)


def solution(mesh):
    one, two, three = P(("gx", "gy")), P(("gx", "gy"), None), P(("gx", "gy"), None, None)
    return jax.shard_map(
        local,
        mesh=mesh,
        in_specs=(three, three, one, two),
        out_specs=(three, three),
        check_vma=False,
    )
```
